128 devices in a mesh: ctx: 16 (over y, z), head: 8 (over x, core).
Axes of the slice: x: 4, y: 4, z: 4, core: 2. Of those that a mesh axis runs over, the one named last changes fastest.
Arguments:
- queries: bfloat16 [16384, 32, 128], P('ctx', 'head'), may hold values from -16 to 16
- keys: bfloat16 [16384, 32, 128], P('ctx', 'head'), may hold values from -16 to 16
- values: bfloat16 [16384, 32, 128], P('ctx', 'head'), may hold values from -6 to 6
- out_grad: bfloat16 [16384, 4096], P('ctx'), may hold values from -6 to 6
- wo: bfloat16 [4096, 4096], P('head', 'ctx'), may hold values from -0.125 to 0.125
Outputs:
- layer_out: bfloat16 [16384, 4096], P('ctx', 'head')
- queries_gradient: bfloat16 [16384, 32, 128], P('ctx', 'head')
- keys_gradient: bfloat16 [16384, 32, 128], P('ctx', 'head')
- values_gradient: bfloat16 [16384, 32, 128], P('ctx', 'head')
- proj_grad: bfloat16 [4096, 4096], P('head', 'ctx')
The draws below stay inside these ranges and needn't reach their ends.
All inputs are finite; a program needn't handle non-finite values.
Results may differ from the reference program's by a relative error of at most 0.015.
Values may be sent and summed in bfloat16 or wider, within the bound.
A program may use at most 128 MiB of HBM per device.

```python
import jax
import jax.numpy as jnp
from jax import lax

D = 4096
H = 32
HS = 128
C = 512
R = 32
L = 16384


def draw_queries(key, part):
    shape = (R * C, H, HS)
    result = jnp.clip(jax.random.normal(jax.random.fold_in(key, 21), shape, jnp.float32), -6.0, 6.0)
    return result.astype(jnp.bfloat16)


def draw_keys(key, part):
    shape = (R * C, H, HS)
    result = jnp.clip(jax.random.normal(jax.random.fold_in(key, 22), shape, jnp.float32), -6.0, 6.0)
    return result.astype(jnp.bfloat16)


def strengthened(drawn, rng, source, target, shards_of, factor):
    def block_of(dim):
        return (jnp.arange(drawn.shape[dim]) // (drawn.shape[dim] // shards_of)).reshape((-1,) + (1,) * (drawn.ndim - 1 - dim))

    near = jax.random.permutation(rng, shards_of)[block_of(target)]
    other_side = (block_of(target) + shards_of // 2) % shards_of
    return jnp.where((block_of(source) == near) | (block_of(source) == other_side), factor * drawn, drawn)


def block_levels(own_key, extent, pieces, low, high):
    def one(dim, parts):
        heights = jax.random.uniform(jax.random.fold_in(jax.random.fold_in(own_key, 6), dim), (parts,), jnp.float32, low / len(pieces), high / len(pieces))
        return jnp.repeat(jnp.exp(heights), extent[dim] // parts).reshape((-1,) + (1,) * (len(extent) - dim - 1))

    factor_of = one(*pieces[0])
    for cut in pieces[1:]:
        factor_of = factor_of * one(*cut)
    return factor_of


def centred(key, shape, width, reach, cuts=(), kind=jnp.bfloat16):
    level = block_levels(key, shape, cuts, -0.22, 0.18) if cuts else 1.0
    values = jax.random.normal(key, shape, jnp.float32) * width * level
    return jnp.minimum(jnp.maximum(values, -reach), reach).astype(kind)


def gaussian_with(stream_key, extent, scale, reach, shards, heavy, kind=jnp.bfloat16):
    drawn = scale * jax.random.normal(stream_key, extent, jnp.float32)
    if shards:
        drawn = drawn * block_levels(stream_key, extent, shards, -0.22, 0.18)
    return jnp.clip(strengthened(drawn, jax.random.fold_in(stream_key, 3), *heavy), -reach, reach).astype(kind)


def setup_inputs(seed: int = 0) -> dict:
    key_list = jax.random.split(jax.random.key(seed), 6)
    return {
        "queries": draw_queries(jax.random.fold_in(key_list[5], 71), 0),
        "keys": draw_keys(jax.random.fold_in(key_list[5], 71), 0),
        "values": centred(key_list[2], (L, H, HS), 1.0, 6.0, ((0, 16), (1, 8))),
        "out_grad": gaussian_with(key_list[3], (L, D), 1.0, 6.0, ((0, 16),), (0, 1, 16, 2.0)),
        "wo": gaussian_with(key_list[4], (H * HS, D), (H * HS) ** -0.5, 0.125, ((0, 8), (1, 16)), (0, 1, 16, 2.0)),
    }


def attend(block_queries, block_keys, block_values, block_gradient):
    scale_factor = HS ** -0.5
    length = block_queries.shape[1]
    places = jnp.arange(length)
    visible = places[:, None] >= places[None, :]
    wide_queries = block_queries.astype(jnp.float32)
    wide_keys = block_keys.astype(jnp.float32)
    wide_values = block_values.astype(jnp.float32)
    wide_gradient = block_gradient.astype(jnp.float32)
    score_matrix = jnp.einsum("osl,ocl->osc", wide_queries, wide_keys) * scale_factor
    score_matrix = jnp.where(visible[None], score_matrix, -jnp.inf)
    highest = jnp.max(score_matrix, axis=-1, keepdims=True)
    lifted = jnp.exp(score_matrix - highest)
    weights = lifted / jnp.sum(lifted, axis=-1, keepdims=True)
    rounded_scores = weights.astype(jnp.bfloat16).astype(jnp.float32)
    attended_values = jnp.einsum("rti,ric->rtc", rounded_scores, wide_values).astype(jnp.bfloat16)
    probability_gradient = jnp.einsum("osl,ocl->osc", wide_gradient, wide_values)
    score_grad = weights * (probability_gradient - jnp.sum(weights * probability_gradient, axis=-1, keepdims=True))
    scores_lowered = score_grad.astype(jnp.bfloat16).astype(jnp.float32)
    queries_gradient = (jnp.einsum("rti,ric->rtc", scores_lowered, wide_keys) * scale_factor).astype(jnp.bfloat16)
    keys_gradient = (jnp.einsum("hfa,hfz->haz", scores_lowered, wide_queries) * scale_factor).astype(jnp.bfloat16)
    values_gradient = jnp.einsum("hfa,hfz->haz", rounded_scores, wide_gradient).astype(jnp.bfloat16)
    return attended_values, queries_gradient, keys_gradient, values_gradient


def row_heads(grids):
    moved = tuple(tensor[:, :, :, 0].transpose(0, 2, 1, 3) for tensor in grids)

    def one_row(row_items):
        return attend(row_items[0], row_items[1], row_items[2], row_items[3])

    results = lax.map(one_row, moved)
    return tuple(tensor.transpose(0, 2, 1, 3) for tensor in results)


def strided_heads(grids):
    half = H // 2
    moved = tuple(tensor[:, :, :, 1].transpose(1, 2, 0, 3).reshape(C * half, R, HS) for tensor in grids)
    results = attend(moved[0], moved[1], moved[2], moved[3])
    return tuple(tensor.reshape(C, half, R, HS).transpose(2, 0, 1, 3) for tensor in results)


def reference(queries, keys, values, out_grad, wo):
    attn_grad = jnp.dot(out_grad, wo.T, preferred_element_type=jnp.float32).astype(jnp.bfloat16)
    attn_grad = attn_grad.reshape(R * C, H, HS)
    grids = tuple(tensor.reshape(R, C, H // 2, 2, HS) for tensor in (queries, keys, values, attn_grad))
    row_parts = row_heads(grids)
    col_parts = strided_heads(grids)
    joined = tuple(jnp.stack([row_parts[index], col_parts[index]], axis=3).reshape(R * C, H, HS) for index in range(4))
    flat_attn = joined[0].reshape(R * C, H * HS)
    layer_out = jnp.dot(flat_attn, wo, preferred_element_type=jnp.float32).astype(jnp.bfloat16)
    proj_grad = jnp.dot(flat_attn.T, out_grad, preferred_element_type=jnp.float32).astype(jnp.bfloat16)
    return layer_out, joined[1], joined[2], joined[3], proj_grad
```

```python
import jax
import jax.numpy as jnp
from jax import lax
from jax.experimental import pallas as pl
from jax.experimental.pallas import tpu as pltpu
from jax.sharding import PartitionSpec as P

MESH = pl.DeviceIdType.MESH
BF16 = jnp.bfloat16
F32 = jnp.float32
SCALE = 128 ** -0.5
SEVEN = tuple((dy, dz) for dy in range(4) for dz in range(4) if dy or dz)


def nt(a, b):
    return lax.dot_general(a, b, (((1,), (1,)), ((), ())), preferred_element_type=F32)


def nn(a, b):
    return lax.dot_general(a, b, (((1,), (0,)), ((), ())), preferred_element_type=F32)


def tn(a, b):
    return lax.dot_general(a, b, (((0,), (0,)), ((), ())), preferred_element_type=F32)


def softmax(scores, visible):
    scores = jnp.where(visible, scores * SCALE, -jnp.inf)
    lifted = jnp.exp(scores - jnp.max(scores, axis=-1, keepdims=True))
    return lifted / jnp.sum(lifted, axis=-1, keepdims=True)


def score_gradient(p, dp):
    return (p * (dp - jnp.sum(p * dp, axis=-1, keepdims=True))).astype(BF16)


def kernel(
    qr, kr, vr, qs, ks, vs, og_hbm, wo_hbm,
    lay_out, dqr, dkr, dvr, dqs, dks, dvs, pg_out,
    W, OG, QKVR, REC, RDO, SO, RO, SDO, SG, PC, PR, ATT, ATTT, AGF, AGR, PP, R1, S2, R2, LS, LR, LX, DR, PG,
    loc, qkv_s, qkv_r, o_s, o_r, do_s, do_r, dg_s, dg_r, w1_s, w1_r, wa_s, wa_r, wb_s, wb_r,
    p1_s, p1_r, p2_s, p2_r, lp_s, lp_r, lx_s, lx_r,
):
    c = lax.axis_index("ctx")
    h = lax.axis_index("head")
    y, z = c // 4, lax.rem(c, 4)
    x, core = h // 2, lax.rem(h, 2)

    def grid_peer(dy, dz):
        return lax.rem(y + dy, 4) * 4 + lax.rem(z + dz, 4)

    def x_head(dx):
        return lax.rem(x + dx, 4) * 2 + core

    partner = (c, x * 2 + (1 - core))

    def remote(src, dst, ssem, rsem, dev):
        return pltpu.make_async_remote_copy(
            src_ref=src, dst_ref=dst, send_sem=ssem, recv_sem=rsem, device_id=dev, device_id_type=MESH
        )

    sends = []

    def push(copy):
        copy.start()
        sends.append(copy)
        return copy

    own_cols = pl.ds(pl.multiple_of(c * 256, 256), 256)

    loads_w = []
    for slot, j in enumerate((0, 2, 1, 3)):
        copy = pltpu.make_async_copy(
            wo_hbm.at[pl.ds(j * 128, 128)], W.at[pl.ds(slot * 128, 128), own_cols], loc.at[slot]
        )
        copy.start()
        loads_w.append(copy)
    loads_r = []
    for t, src in enumerate((qr, kr, vr)):
        copy = pltpu.make_async_copy(src, QKVR.at[t], loc.at[4 + t])
        copy.start()
        loads_r.append(copy)
    loads_s = []
    for t, src in enumerate((qs, ks, vs)):
        copy = pltpu.make_async_copy(src.at[c], REC.at[t, c], loc.at[7 + t])
        copy.start()
        loads_s.append(copy)
    load_og = pltpu.make_async_copy(og_hbm, OG, loc.at[10])
    load_og.start()

    barrier = pltpu.get_barrier_semaphore()
    for dy, dz in SEVEN:
        pl.semaphore_signal(barrier, inc=1, device_id=(grid_peer(dy, dz), h), device_id_type=MESH)
    for dx in range(1, 4):
        pl.semaphore_signal(barrier, inc=1, device_id=(c, x_head(dx)), device_id_type=MESH)
    pl.semaphore_signal(barrier, inc=1, device_id=partner, device_id_type=MESH)
    pl.semaphore_wait(barrier, 19)

    qkv_in = []
    for t, src in enumerate((qs, ks, vs)):
        for i, (dy, dz) in enumerate(SEVEN):
            to = grid_peer(dy, dz)
            qkv_in.append(push(remote(src.at[to], REC.at[t, c], qkv_s.at[t, i], qkv_r.at[t, i], (to, h))))

    for copy in loads_w:
        copy.wait()
    w_own = W.at[:, own_cols]
    wz, wy = [], []
    for d in range(1, 4):
        wz.append(push(remote(w_own, w_own, w1_s.at[d - 1], w1_r.at[d - 1], (grid_peer(0, d), h))))
        wy.append(push(remote(w_own, w_own, w1_s.at[2 + d], w1_r.at[2 + d], (grid_peer(d, 0), h))))

    for copy in loads_r:
        copy.wait()

    def causal(rows, cols, first):
        return (
            lax.broadcasted_iota(jnp.int32, (rows, cols), 0) + first
            >= lax.broadcasted_iota(jnp.int32, (rows, cols), 1)
        )

    def row_forward(i, carry):
        r, hh = i // 2, lax.rem(i, 2)
        lanes = pl.ds(pl.multiple_of(hh * 128, 128), 128)
        for b in range(2):
            n = 256 * (b + 1)
            q = QKVR[0, i, pl.ds(256 * b, 256), :]
            p = softmax(nt(q, QKVR[1, i, pl.ds(0, n), :]), causal(256, n, 256 * b))
            PR[i, pl.ds(256 * b, 256), pl.ds(0, n)] = p
            o = nn(p.astype(BF16), QKVR[2, i, pl.ds(0, n), :])
            rows = pl.ds(pl.multiple_of(r * 512 + 256 * b, 256), 256)
            ATT[rows, lanes] = o.astype(BF16)
            ATTT[lanes, rows] = o.T.astype(BF16)
        return carry

    lax.fori_loop(0, 4, row_forward, 0)

    def projection(half):
        def one(n, carry):
            cols = pl.ds(pl.multiple_of(n * 256, 256), 256)
            part = nn(ATTT[pl.ds(256 * half, 256), :], OG[:, cols])
            PP[half, n // 4, lax.rem(n, 4)] = part.astype(BF16)
            return carry

        lax.fori_loop(0, 16, one, 0)

    load_og.wait()
    projection(0)

    for copy in qkv_in:
        copy.wait_recv()
    for copy in loads_s:
        copy.wait()
    ii = lax.broadcasted_iota(jnp.int32, (256, 256), 0)
    jj = lax.broadcasted_iota(jnp.int32, (256, 256), 1)

    def tile(ref):
        return ref.reshape(256, 128)

    def col_forward(i, carry):
        hh, g = i // 4, lax.rem(i, 4)
        visible = (lax.rem(ii, 8) == lax.rem(jj, 8)) & (ii >= jj)
        p = softmax(nt(tile(REC[0, :, hh, g]), tile(REC[1, :, hh, g])), visible)
        PC[i] = p
        o = nn(p.astype(BF16), tile(REC[2, :, hh, g]))
        SO[:, hh, g] = o.astype(BF16).reshape(16, 16, 128)
        return carry

    lax.fori_loop(0, 8, col_forward, 0)
    o_in = []
    for i, (dy, dz) in enumerate(SEVEN):
        to = grid_peer(dy, dz)
        o_in.append(push(remote(SO.at[to], RO.at[c], o_s.at[i], o_r.at[i], (to, h))))
    RO[c] = SO[c]

    wa, wb = [], []
    for d in range(1, 4):
        wz[d - 1].wait_recv()
        block = W.at[pl.ds(0, 256), pl.ds(pl.multiple_of(grid_peer(0, 4 - d) * 256, 256), 256)]
        for e in range(1, 4):
            k = 3 * (d - 1) + e - 1
            wa.append(push(remote(block, block, wa_s.at[k], wa_r.at[k], (grid_peer(e, 0), h))))
        wy[d - 1].wait_recv()
        block = W.at[pl.ds(256, 256), pl.ds(pl.multiple_of(grid_peer(4 - d, 0) * 256, 256), 256)]
        for e in range(1, 4):
            k = 3 * (d - 1) + e - 1
            wb.append(push(remote(block, block, wb_s.at[k], wb_r.at[k], (grid_peer(0, e), h))))

    for copy in o_in:
        copy.wait_recv()
    for hh in range(2):
        for g in range(4):
            block = RO[:, hh, g].astype(F32)
            for r in range(2):
                AGF[r, :, g, :, pl.ds(hh * 128, 128)] = block[:, 8 * r : 8 * r + 8, :]

    def place(m, carry):
        block = AGF[m // 2, pl.ds(pl.multiple_of(lax.rem(m, 2) * 8, 8), 8)].reshape(256, 256)
        rows = pl.ds(pl.multiple_of(m * 256, 256), 256)
        ATT[rows, pl.ds(256, 256)] = block.astype(BF16)
        ATTT[pl.ds(256, 256), rows] = block.T.astype(BF16)
        return carry

    lax.fori_loop(0, 4, place, 0)
    projection(1)

    for copy in wb:
        copy.wait_recv()
    for copy in wa:
        copy.wait_recv()

    def strided_cotangent(m, carry):
        rows = pl.ds(pl.multiple_of(m * 256, 256), 256)
        part = nt(OG[rows, :], W[pl.ds(256, 256), :])
        AGF[m // 2, pl.ds(pl.multiple_of(lax.rem(m, 2) * 8, 8), 8)] = part.reshape(8, 4, 8, 256)
        return carry

    lax.fori_loop(0, 4, strided_cotangent, 0)
    for hh in range(2):
        for g in range(4):
            lanes = pl.ds(hh * 128, 128)
            both = jnp.concatenate([AGF[0, :, g, :, lanes], AGF[1, :, g, :, lanes]], axis=1)
            SDO[:, hh, g] = both.astype(BF16)
    do_in = []
    for i, (dy, dz) in enumerate(SEVEN):
        to = grid_peer(dy, dz)
        do_in.append(push(remote(SDO.at[to], RDO.at[c], do_s.at[i], do_r.at[i], (to, h))))
    RDO[c] = SDO[c]

    p1_in = []
    for d in range(1, 4):
        to = lax.rem(z + d, 4)
        p1_in.append(
            push(remote(PP.at[0, :, to], R1.at[0, d - 1], p1_s.at[0, d - 1], p1_r.at[0, d - 1], (grid_peer(0, d), h)))
        )
        to = lax.rem(y + d, 4)
        p1_in.append(
            push(remote(PP.at[1, to], R1.at[1, d - 1], p1_s.at[1, d - 1], p1_r.at[1, d - 1], (grid_peer(d, 0), h)))
        )

    def partial_out(m, head):
        rows = pl.ds(pl.multiple_of(m * 256, 256), 256)
        cols = pl.ds(pl.multiple_of(head * 512, 512), 512)
        return rows, nn(ATT[rows, :], W[:, cols])

    lp_in = []
    for n, dx in enumerate((2, 1, 3, 0)):
        head = lax.rem(x + dx, 4) * 2 + (1 - core)

        def for_partner(m, carry, n=n, head=head):
            rows, part = partial_out(m, head)
            LS[n, rows, :] = part.astype(BF16)
            return carry

        lax.fori_loop(0, 4, for_partner, 0)
        lp_in.append(push(remote(LS.at[n], LR.at[n], lp_s.at[n], lp_r.at[n], partner)))

    lx_in = []
    for n, dx in enumerate((2, 1, 3, 0)):
        head = x_head(dx)
        lp_in[n].wait_recv()

        def for_x(m, carry, n=n, head=head):
            rows, part = partial_out(m, head)
            LR[n, rows, :] = (part + LR[n, rows, :].astype(F32)).astype(BF16)
            return carry

        lax.fori_loop(0, 4, for_x, 0)
        if dx:
            lx_in.append(push(remote(LR.at[n], LX.at[n], lx_s.at[n], lx_r.at[n], (c, head))))

    for copy in do_in:
        copy.wait_recv()

    def col_backward(i, carry):
        hh, g = i // 4, lax.rem(i, 4)
        p = PC[i]
        grad = tile(RDO[:, hh, g])
        low = score_gradient(p, nt(grad, tile(REC[2, :, hh, g])))
        SG[0, :, hh, g] = (nn(low, tile(REC[1, :, hh, g])) * SCALE).astype(BF16).reshape(16, 16, 128)
        SG[1, :, hh, g] = (tn(low, tile(REC[0, :, hh, g])) * SCALE).astype(BF16).reshape(16, 16, 128)
        SG[2, :, hh, g] = tn(p.astype(BF16), grad).astype(BF16).reshape(16, 16, 128)
        return carry

    lax.fori_loop(0, 8, col_backward, 0)
    dg_in = []
    stores = []
    for t, dst in enumerate((dqs, dks, dvs)):
        for i, (dy, dz) in enumerate(SEVEN):
            to = grid_peer(dy, dz)
            dg_in.append(push(remote(SG.at[t, to], dst.at[c], dg_s.at[t, i], dg_r.at[t, i], (to, h))))
        copy = pltpu.make_async_copy(SG.at[t, c], dst.at[c], loc.at[11 + t])
        copy.start()
        stores.append(copy)

    def row_cotangent(m, carry):
        rows = pl.ds(pl.multiple_of(m * 256, 256), 256)
        AGR[rows, :] = nt(OG[rows, :], W[pl.ds(0, 256), :]).astype(BF16)
        return carry

    lax.fori_loop(0, 4, row_cotangent, 0)

    def row_backward(i, carry):
        r, hh = i // 2, lax.rem(i, 2)
        lanes = pl.ds(pl.multiple_of(hh * 128, 128), 128)
        for b in range(2):
            n = 256 * (b + 1)
            rows = pl.ds(256 * b, 256)
            seen = pl.ds(0, n)
            p = PR[i, rows, seen]
            grad = AGR[pl.ds(pl.multiple_of(r * 512 + 256 * b, 256), 256), lanes]
            low = score_gradient(p, nt(grad, QKVR[2, i, seen, :]))
            DR[0, i, rows, :] = (nn(low, QKVR[1, i, seen, :]) * SCALE).astype(BF16)
            dk = tn(low, QKVR[0, i, rows, :])
            dv = tn(p.astype(BF16), grad)
            if b == 0:
                dk_first, dv_first = dk, dv
            else:
                DR[1, i, pl.ds(0, 256), :] = ((dk[:256] + dk_first) * SCALE).astype(BF16)
                DR[1, i, pl.ds(256, 256), :] = (dk[256:] * SCALE).astype(BF16)
                DR[2, i, pl.ds(0, 256), :] = (dv[:256] + dv_first).astype(BF16)
                DR[2, i, pl.ds(256, 256), :] = dv[256:].astype(BF16)
        return carry

    lax.fori_loop(0, 4, row_backward, 0)
    for t, dst in enumerate((dqr, dkr, dvr)):
        copy = pltpu.make_async_copy(DR.at[t], dst, loc.at[14 + t])
        copy.start()
        stores.append(copy)

    for copy in p1_in:
        copy.wait_recv()
    p2_in = []
    for half in range(2):
        for d in (1, 2, 3, 0):
            if half == 0:
                other = lax.rem(y + d, 4)
                total = PP[0, other, z].astype(F32)
                dev = (grid_peer(d, 0), h)
            else:
                other = lax.rem(z + d, 4)
                total = PP[1, y, other].astype(F32)
                dev = (grid_peer(0, d), h)
            for k in range(3):
                total = total + R1[half, k, other].astype(F32)
            S2[half, d] = total.astype(BF16)
            if d:
                p2_in.append(
                    push(remote(S2.at[half, d], R2.at[half, d - 1], p2_s.at[half, d - 1], p2_r.at[half, d - 1], dev))
                )

    for copy in lx_in:
        copy.wait_recv()

    def finish(m, carry):
        rows = pl.ds(pl.multiple_of(m * 256, 256), 256)
        total = LR[3, rows, :].astype(F32)
        for k in range(3):
            total = total + LX[k, rows, :].astype(F32)
        LX[0, rows, :] = total.astype(BF16)
        return carry

    lax.fori_loop(0, 4, finish, 0)
    copy = pltpu.make_async_copy(LX.at[0], lay_out, loc.at[17])
    copy.start()
    stores.append(copy)

    for copy in p2_in:
        copy.wait_recv()
    for half in range(2):
        total = S2[half, 0].astype(F32)
        for k in range(3):
            total = total + R2[half, k].astype(F32)
        PG[half] = total.astype(BF16)
        for hh in range(2):
            copy = pltpu.make_async_copy(
                PG.at[half, pl.ds(hh * 128, 128)], pg_out.at[pl.ds((2 * hh + half) * 128, 128)], loc.at[18 + 2 * half + hh]
            )
            copy.start()
            stores.append(copy)

    for copy in dg_in:
        copy.wait_recv()
    for copy in stores:
        copy.wait()
    for copy in sends:
        copy.wait_send()


def on_device(queries, keys, values, out_grad, wo):
    def split(tensor):
        grid = tensor.reshape(2, 16, 4, 8, 2, 2, 128)
        row = grid[:, :, :, :, :, 0].transpose(0, 4, 1, 2, 3, 5).reshape(4, 512, 128)
        strided = grid[:, :, :, :, :, 1].transpose(1, 4, 2, 0, 3, 5).reshape(16, 2, 4, 16, 128)
        return row, strided

    def join(row, strided):
        row = row.reshape(2, 2, 16, 4, 8, 128).transpose(0, 2, 3, 4, 1, 5)
        strided = strided.reshape(16, 2, 4, 2, 8, 128).transpose(3, 0, 2, 4, 1, 5)
        return jnp.stack([row, strided], axis=5).reshape(1024, 4, 128)

    rows, strided = zip(*(split(t) for t in (queries, keys, values)))
    row_shape = jax.ShapeDtypeStruct((4, 512, 128), BF16)
    strided_shape = jax.ShapeDtypeStruct((16, 2, 4, 16, 128), BF16)
    any_spec = pl.BlockSpec(memory_space=pl.ANY)

    def vmem(*shape, dtype=BF16):
        return pltpu.VMEM(shape, dtype)

    def sems(*shape):
        return pltpu.SemaphoreType.DMA(shape)

    out = pl.pallas_call(
        kernel,
        name="layer",
        out_shape=(
            jax.ShapeDtypeStruct((1024, 512), BF16),
            row_shape, row_shape, row_shape,
            strided_shape, strided_shape, strided_shape,
            jax.ShapeDtypeStruct((512, 256), BF16),
        ),
        in_specs=[any_spec] * 8,
        out_specs=[any_spec] * 8,
        scratch_shapes=[
            vmem(512, 4096),
            vmem(1024, 4096),
            vmem(3, 4, 512, 128),
            vmem(3, 16, 2, 4, 16, 128),
            vmem(16, 2, 4, 16, 128),
            vmem(16, 2, 4, 16, 128),
            vmem(16, 2, 4, 16, 128),
            vmem(16, 2, 4, 16, 128),
            vmem(3, 16, 2, 4, 16, 128),
            vmem(8, 256, 256, dtype=F32),
            vmem(4, 512, 512, dtype=F32),
            vmem(1024, 512),
            vmem(512, 1024),
            vmem(2, 16, 4, 8, 256, dtype=F32),
            vmem(1024, 256),
            vmem(2, 4, 4, 256, 256),
            vmem(2, 3, 4, 256, 256),
            vmem(2, 4, 256, 256),
            vmem(2, 3, 256, 256),
            vmem(4, 1024, 512),
            vmem(4, 1024, 512),
            vmem(3, 1024, 512),
            vmem(3, 4, 512, 128),
            vmem(2, 256, 256),
            sems(22),
            sems(3, 15), sems(3, 15),
            sems(15), sems(15),
            sems(15), sems(15),
            sems(3, 15), sems(3, 15),
            sems(6), sems(6),
            sems(9), sems(9),
            sems(9), sems(9),
            sems(2, 3), sems(2, 3),
            sems(2, 3), sems(2, 3),
            sems(4), sems(4),
            sems(3), sems(3),
        ],
        compiler_params=pltpu.CompilerParams(
            collective_id=0, has_side_effects=True, vmem_limit_bytes=63 << 20
        ),
    )(*rows, *strided, out_grad, wo)
    lay, dqr, dkr, dvr, dqs, dks, dvs, pg = out
    return lay, join(dqr, dqs), join(dkr, dks), join(dvr, dvs), pg


def solution(mesh):
    in_specs = (
        P("ctx", "head", None),
        P("ctx", "head", None),
        P("ctx", "head", None),
        P("ctx", None),
        P("head", "ctx"),
    )
    out_specs = (
        P("ctx", "head"),
        P("ctx", "head", None),
        P("ctx", "head", None),
        P("ctx", "head", None),
        P("head", "ctx"),
    )
    return jax.shard_map(
        on_device, mesh=mesh, in_specs=in_specs, out_specs=out_specs, check_vma=False
    )
```

```python
import jax
import jax.numpy as jnp
from jax import lax
from jax.experimental import pallas as pl
from jax.experimental.pallas import tpu as pltpu
from jax.sharding import PartitionSpec as P

MESH = pl.DeviceIdType.MESH
BF16 = jnp.bfloat16
F32 = jnp.float32
SCALE = 128 ** -0.5
SEVEN = tuple((dy, dz) for dy in range(4) for dz in range(4) if dy or dz)


def nt(a, b):
    return lax.dot_general(a, b, (((1,), (1,)), ((), ())), preferred_element_type=F32)


def nn(a, b):
    return lax.dot_general(a, b, (((1,), (0,)), ((), ())), preferred_element_type=F32)


def tn(a, b):
    return lax.dot_general(a, b, (((0,), (0,)), ((), ())), preferred_element_type=F32)


def softmax(scores, visible):
    scores = jnp.where(visible, scores * SCALE, -jnp.inf)
    lifted = jnp.exp(scores - jnp.max(scores, axis=-1, keepdims=True))
    return lifted / jnp.sum(lifted, axis=-1, keepdims=True)


def score_gradient(p, dp):
    return (p * (dp - jnp.sum(p * dp, axis=-1, keepdims=True))).astype(BF16)


def kernel(
    q_hbm, k_hbm, v_hbm, og_hbm, wo_hbm,
    lay_out, dq_out, dk_out, dv_out, pg_out,
    RAW, WIDE, QS, RDG,
    W, OG, QKVR, REC, RDO, SO, RO, SDO, SG, PC, PR, ATT, ATTT, AGF, AGR, PP, RL, R1, S2, R2, LS, LR, LX, XR, PG,
    loc, qkv_s, qkv_r, o_s, o_r, do_s, do_r, dg_s, dg_r, w1_s, w1_r, wa_s, wa_r, wb_s, wb_r, wc_s, wc_r,
    p1_s, p1_r, p2_s, p2_r, lp_s, lp_r, lx_s, lx_r,
):
    c = lax.axis_index("ctx")
    h = lax.axis_index("head")
    y, z = c // 4, lax.rem(c, 4)
    x, core = h // 2, lax.rem(h, 2)

    def grid_peer(dy, dz):
        return lax.rem(y + dy, 4) * 4 + lax.rem(z + dz, 4)

    def x_head(dx):
        return lax.rem(x + dx, 4) * 2 + core

    partner = (c, x * 2 + (1 - core))

    def remote(src, dst, ssem, rsem, dev):
        return pltpu.make_async_remote_copy(
            src_ref=src, dst_ref=dst, send_sem=ssem, recv_sem=rsem, device_id=dev, device_id_type=MESH
        )

    sends = []

    def push(copy):
        copy.start()
        sends.append(copy)
        return copy

    own_cols = pl.ds(pl.multiple_of(c * 256, 256), 256)

    loads_q = []
    for t, src in enumerate((q_hbm, k_hbm, v_hbm)):
        copy = pltpu.make_async_copy(src, RAW.at[t], loc.at[t])
        copy.start()
        loads_q.append(copy)
    loads_w = []
    for slot, j in enumerate((0, 2, 1, 3)):
        copy = pltpu.make_async_copy(
            wo_hbm.at[pl.ds(j * 128, 128)], W.at[pl.ds(slot * 128, 128), own_cols], loc.at[3 + slot]
        )
        copy.start()
        loads_w.append(copy)
    load_og = pltpu.make_async_copy(og_hbm, OG, loc.at[7])
    load_og.start()

    barrier = pltpu.get_barrier_semaphore()
    for dy, dz in SEVEN:
        pl.semaphore_signal(barrier, inc=1, device_id=(grid_peer(dy, dz), h), device_id_type=MESH)
    for dx in range(1, 4):
        pl.semaphore_signal(barrier, inc=1, device_id=(c, x_head(dx)), device_id_type=MESH)
    pl.semaphore_signal(barrier, inc=1, device_id=partner, device_id_type=MESH)

    def unpack(t):
        loads_q[t].wait()

        def widen(m, carry):
            rows = pl.ds(pl.multiple_of(m * 512, 512), 512)
            WIDE[t, rows, :] = RAW[t, rows, :].astype(F32)
            return carry

        lax.fori_loop(0, 8, widen, 0)

        def strided(m, carry):
            for hh in range(2):
                both = []
                for r in range(2):
                    first = r * 2048 + 2 * hh + 1 + m * 512
                    both.append(WIDE[t, pl.ds(first, 128, stride=4), :].reshape(4, 4, 8, 128))
                QS[t, pl.ds(m * 4, 4), hh] = jnp.concatenate(both, axis=2).astype(BF16)
            return carry

        lax.fori_loop(0, 4, strided, 0)

    unpack(0)
    for copy in loads_w:
        copy.wait()
    pl.semaphore_wait(barrier, 19)

    w_own = W.at[:, own_cols]
    wz, wy = [], []
    for d in range(1, 4):
        wz.append(push(remote(w_own, w_own, w1_s.at[d - 1], w1_r.at[d - 1], (grid_peer(0, d), h))))
        wy.append(push(remote(w_own, w_own, w1_s.at[2 + d], w1_r.at[2 + d], (grid_peer(d, 0), h))))

    qkv_in = []

    def send_strided(t):
        for i, (dy, dz) in enumerate(SEVEN):
            to = grid_peer(dy, dz)
            qkv_in.append(push(remote(QS.at[t, to], REC.at[t, c], qkv_s.at[t, i], qkv_r.at[t, i], (to, h))))
        REC[t, c] = QS[t, c]

    send_strided(0)
    unpack(1)
    send_strided(1)
    unpack(2)
    send_strided(2)

    def w_block(first, size, owner):
        return W.at[pl.ds(first, size), pl.ds(pl.multiple_of(owner * 256, 256), 256)]

    wa = [[None] * 2 for _ in range(3)]
    wb = [[None] * 2 for _ in range(3)]

    def spread_w():
        for d in range(1, 4):
            wz[d - 1].wait_recv()
            block = w_block(0, 256, grid_peer(0, 4 - d))
            for k, e in enumerate((1, 3)):
                wa[d - 1][k] = push(
                    remote(block, block, wa_s.at[d - 1, k], wa_r.at[d - 1, k], (grid_peer(e, 0), h))
                )
            wy[d - 1].wait_recv()
            block = w_block(256, 256, grid_peer(4 - d, 0))
            for k, e in enumerate((1, 3)):
                wb[d - 1][k] = push(
                    remote(block, block, wb_s.at[d - 1, k], wb_r.at[d - 1, k], (grid_peer(0, e), h))
                )

    wc = []

    def relay_w():
        for d in range(1, 4):
            for k, e in enumerate((1, 3)):
                wa[d - 1][k].wait_recv()
                block = w_block(128 * k, 128, grid_peer(4 - e, 4 - d))
                wc.append(push(remote(block, block, wc_s.at[0, d - 1, k], wc_r.at[0, d - 1, k], (grid_peer(e, 0), h))))
                wb[d - 1][k].wait_recv()
                block = w_block(256 + 128 * k, 128, grid_peer(4 - d, 4 - e))
                wc.append(push(remote(block, block, wc_s.at[1, d - 1, k], wc_r.at[1, d - 1, k], (grid_peer(0, e), h))))

    def unpack_rows(m, carry):
        for t in range(3):
            for hh in range(2):
                rows = WIDE[t, pl.ds(m * 512 + 2 * hh, 128, stride=4), :].astype(BF16)
                QKVR[t, (m // 4) * 2 + hh, pl.ds(pl.multiple_of(lax.rem(m, 4) * 128, 128), 128), :] = rows
        return carry

    lax.fori_loop(0, 8, unpack_rows, 0)

    def causal(rows, cols, first):
        return (
            lax.broadcasted_iota(jnp.int32, (rows, cols), 0) + first
            >= lax.broadcasted_iota(jnp.int32, (rows, cols), 1)
        )

    def row_forward(i, carry):
        r, hh = i // 2, lax.rem(i, 2)
        lanes = pl.ds(pl.multiple_of(hh * 128, 128), 128)
        for b in range(2):
            n = 256 * (b + 1)
            q = QKVR[0, i, pl.ds(256 * b, 256), :]
            p = softmax(nt(q, QKVR[1, i, pl.ds(0, n), :]), causal(256, n, 256 * b))
            PR[i, pl.ds(256 * b, 256), pl.ds(0, n)] = p
            o = nn(p.astype(BF16), QKVR[2, i, pl.ds(0, n), :])
            rows = pl.ds(pl.multiple_of(r * 512 + 256 * b, 256), 256)
            ATT[rows, lanes] = o.astype(BF16)
            ATTT[lanes, rows] = o.T.astype(BF16)
        return carry

    lax.fori_loop(0, 4, row_forward, 0)

    def projection(half):
        def one(n, carry):
            cols = pl.ds(pl.multiple_of(n * 256, 256), 256)
            part = nn(ATTT[pl.ds(256 * half, 256), :], OG[:, cols])
            for q in range(2):
                PP[2 * half + q, n // 4, lax.rem(n, 4)] = part[128 * q : 128 * q + 128].astype(BF16)
            return carry

        lax.fori_loop(0, 16, one, 0)

    spread_w()
    load_og.wait()
    projection(0)

    first_half, second_half = pl.ds(0, 2), pl.ds(2, 2)

    def group(q, d, part):
        if q % 2 == 0:
            return PP.at[q, part, lax.rem(z + d, 4)]
        return PP.at[q, lax.rem(y + d, 4), part]

    def along(q, d, second=False):
        return (grid_peer(0, d) if (q % 2 == 0) != second else grid_peer(d, 0), h)

    pr_in, p1_in, p2_in = [None] * 4, [None] * 4, [None] * 4

    def reduce_start(q):
        pr_in[q] = [
            push(remote(group(q, 2, first_half), RL.at[q, 0], p1_s.at[q, 0], p1_r.at[q, 0], along(q, 1))),
            push(remote(group(q, 2, second_half), RL.at[q, 1], p1_s.at[q, 1], p1_r.at[q, 1], along(q, 3))),
        ]
        p1_in[q] = [
            push(remote(group(q, 1, second_half), R1.at[q, 0, second_half], p1_s.at[q, 2], p1_r.at[q, 2], along(q, 1))),
            push(remote(group(q, 3, first_half), R1.at[q, 1, first_half], p1_s.at[q, 3], p1_r.at[q, 3], along(q, 3))),
        ]

    def reduce_pass(q):
        for k, (d, part) in enumerate(((1, first_half), (3, second_half))):
            pr_in[q][k].wait_recv()
            mine = group(q, d, part)
            mine[...] = (mine[...].astype(F32) + RL[q, k].astype(F32)).astype(BF16)
            p1_in[q].append(
                push(remote(mine, R1.at[q, k, part], p1_s.at[q, 4 + k], p1_r.at[q, 4 + k], along(q, d)))
            )

    def reduce_middle(q):
        for copy in p1_in[q]:
            copy.wait_recv()
        p2_in[q] = []
        for d in (2, 1, 3, 0):
            if q % 2 == 0:
                other = lax.rem(y + d, 4)
                mine = PP[q, other, z]
            else:
                other = lax.rem(z + d, 4)
                mine = PP[q, y, other]
            total = mine.astype(F32) + R1[q, 0, other].astype(F32) + R1[q, 1, other].astype(F32)
            S2[q, d] = total.astype(BF16)
            if d:
                p2_in[q].append(
                    push(remote(S2.at[q, d], R2.at[q, d - 1], p2_s.at[q, d - 1], p2_r.at[q, d - 1], along(q, d, True)))
                )

    def reduce_end(q):
        for copy in p2_in[q]:
            copy.wait_recv()
        total = S2[q, 0].astype(F32)
        for k in range(3):
            total = total + R2[q, k].astype(F32)
        PG[q] = total.astype(BF16)
        copy = pltpu.make_async_copy(PG.at[q], pg_out.at[pl.ds((2 * (q % 2) + q // 2) * 128, 128)], loc.at[12 + q])
        copy.start()
        stores.append(copy)

    for copy in qkv_in:
        copy.wait_recv()
    ii = lax.broadcasted_iota(jnp.int32, (256, 256), 0)
    jj = lax.broadcasted_iota(jnp.int32, (256, 256), 1)

    def tile(ref):
        return ref.reshape(256, 128)

    def col_forward(i, carry):
        hh, g = i // 4, lax.rem(i, 4)
        visible = (lax.rem(ii, 8) == lax.rem(jj, 8)) & (ii >= jj)
        p = softmax(nt(tile(REC[0, :, hh, g]), tile(REC[1, :, hh, g])), visible)
        PC[i] = p
        o = nn(p.astype(BF16), tile(REC[2, :, hh, g]))
        SO[:, hh, g] = o.astype(BF16).reshape(16, 16, 128)
        return carry

    lax.fori_loop(0, 8, col_forward, 0, unroll=2)
    o_in = []
    for i, (dy, dz) in enumerate(SEVEN):
        to = grid_peer(dy, dz)
        o_in.append(push(remote(SO.at[to], RO.at[c], o_s.at[i], o_r.at[i], (to, h))))
    RO[c] = SO[c]

    relay_w()
    reduce_start(0)
    reduce_start(1)

    for copy in o_in:
        copy.wait_recv()
    for hh in range(2):
        for g in range(4):
            block = RO[:, hh, g].astype(F32)
            for r in range(2):
                AGF[r, :, g, :, pl.ds(hh * 128, 128)] = block[:, 8 * r : 8 * r + 8, :]

    def place(m, carry):
        block = AGF[m // 2, pl.ds(pl.multiple_of(lax.rem(m, 2) * 8, 8), 8)].reshape(256, 256)
        rows = pl.ds(pl.multiple_of(m * 256, 256), 256)
        ATT[rows, pl.ds(256, 256)] = block.astype(BF16)
        ATTT[pl.ds(256, 256), rows] = block.T.astype(BF16)
        return carry

    lax.fori_loop(0, 4, place, 0)
    projection(1)

    for copy in wc:
        copy.wait_recv()

    def strided_cotangent(m, carry):
        rows = pl.ds(pl.multiple_of(m * 256, 256), 256)
        part = nt(OG[rows, :], W[pl.ds(256, 256), :])
        AGF[m // 2, pl.ds(pl.multiple_of(lax.rem(m, 2) * 8, 8), 8)] = part.reshape(8, 4, 8, 256)
        return carry

    lax.fori_loop(0, 4, strided_cotangent, 0)
    for hh in range(2):
        for g in range(4):
            lanes = pl.ds(hh * 128, 128)
            both = jnp.concatenate([AGF[0, :, g, :, lanes], AGF[1, :, g, :, lanes]], axis=1)
            SDO[:, hh, g] = both.astype(BF16)
    do_in = []
    for i, (dy, dz) in enumerate(SEVEN):
        to = grid_peer(dy, dz)
        do_in.append(push(remote(SDO.at[to], RDO.at[c], do_s.at[i], do_r.at[i], (to, h))))
    RDO[c] = SDO[c]
    reduce_start(2)
    reduce_start(3)
    reduce_pass(0)
    reduce_pass(1)

    def partial_out(m, head):
        rows = pl.ds(pl.multiple_of(m * 256, 256), 256)
        cols = pl.ds(pl.multiple_of(head * 512, 512), 512)
        return rows, nn(ATT[rows, :], W[:, cols])

    order = (2, 1, 3, 0)
    lp_in = [None] * 4

    def to_partner(n):
        head = lax.rem(x + order[n], 4) * 2 + (1 - core)

        def for_partner(m, carry):
            rows, part = partial_out(m, head)
            LS[n, rows, :] = part.astype(BF16)
            return carry

        lax.fori_loop(0, 4, for_partner, 0)
        lp_in[n] = push(remote(LS.at[n], LR.at[n], lp_s.at[n], lp_r.at[n], partner))

    def to_x(n):
        head = x_head(order[n])
        lp_in[n].wait_recv()

        def for_x(m, carry):
            rows, part = partial_out(m, head)
            LR[n, rows, :] = (part + LR[n, rows, :].astype(F32)).astype(BF16)
            return carry

        lax.fori_loop(0, 4, for_x, 0)

    lower, upper = pl.ds(0, 512), pl.ds(512, 512)
    ahead, behind = (c, x_head(1)), (c, x_head(3))

    def add_passing(n, k, rows):
        relay[k].wait_recv()
        LR[n, rows, :] = (LR[n, rows, :].astype(F32) + XR[k].astype(F32)).astype(BF16)

    to_partner(0)
    to_partner(1)
    to_x(0)
    relay = [
        push(remote(LR.at[0, lower], XR.at[0], lx_s.at[0], lx_r.at[0], ahead)),
        push(remote(LR.at[0, upper], XR.at[1], lx_s.at[1], lx_r.at[1], behind)),
    ]
    to_partner(2)
    to_x(1)
    lx_in = [push(remote(LR.at[1, upper], LX.at[0, upper], lx_s.at[2], lx_r.at[2], ahead))]
    to_partner(3)
    to_x(2)
    lx_in.append(push(remote(LR.at[2, lower], LX.at[1, lower], lx_s.at[3], lx_r.at[3], behind)))

    for copy in do_in:
        copy.wait_recv()

    def col_backward(i, carry):
        hh, g = i // 4, lax.rem(i, 4)
        p = PC[i]
        grad = tile(RDO[:, hh, g])
        low = score_gradient(p, nt(grad, tile(REC[2, :, hh, g])))
        SG[0, :, hh, g] = (nn(low, tile(REC[1, :, hh, g])) * SCALE).astype(BF16).reshape(16, 16, 128)
        SG[1, :, hh, g] = (tn(low, tile(REC[0, :, hh, g])) * SCALE).astype(BF16).reshape(16, 16, 128)
        SG[2, :, hh, g] = tn(p.astype(BF16), grad).astype(BF16).reshape(16, 16, 128)
        return carry

    lax.fori_loop(0, 8, col_backward, 0, unroll=2)
    reduce_pass(2)
    reduce_pass(3)
    dg_in = []
    stores = []
    for t in range(3):
        for i, (dy, dz) in enumerate(SEVEN):
            to = grid_peer(dy, dz)
            dg_in.append(push(remote(SG.at[t, to], RDG.at[t, c], dg_s.at[t, i], dg_r.at[t, i], (to, h))))
        RDG[t, c] = SG[t, c]

    to_x(3)
    add_passing(1, 0, lower)
    lx_in.append(push(remote(LR.at[1, lower], LX.at[0, lower], lx_s.at[4], lx_r.at[4], ahead)))
    add_passing(2, 1, upper)
    lx_in.append(push(remote(LR.at[2, upper], LX.at[1, upper], lx_s.at[5], lx_r.at[5], behind)))

    reduce_middle(0)
    reduce_middle(1)
    reduce_middle(2)
    reduce_middle(3)

    def row_cotangent(m, carry):
        rows = pl.ds(pl.multiple_of(m * 256, 256), 256)
        AGR[rows, :] = nt(OG[rows, :], W[pl.ds(0, 256), :]).astype(BF16)
        return carry

    lax.fori_loop(0, 4, row_cotangent, 0)

    def row_backward(i, carry):
        r, hh = i // 2, lax.rem(i, 2)
        lanes = pl.ds(pl.multiple_of(hh * 128, 128), 128)
        for b in range(2):
            n = 256 * (b + 1)
            rows = pl.ds(256 * b, 256)
            seen = pl.ds(0, n)
            p = PR[i, rows, seen]
            grad = AGR[pl.ds(pl.multiple_of(r * 512 + 256 * b, 256), 256), lanes]
            low = score_gradient(p, nt(grad, QKVR[2, i, seen, :]))
            first = r * 2048 + 2 * hh
            WIDE[0, pl.ds(first + 1024 * b, 256, stride=4), :] = nn(low, QKVR[1, i, seen, :]) * SCALE
            dk = tn(low, QKVR[0, i, rows, :])
            dv = tn(p.astype(BF16), grad)
            if b == 0:
                dk_first, dv_first = dk, dv
            else:
                WIDE[1, pl.ds(first, 256, stride=4), :] = (dk[:256] + dk_first) * SCALE
                WIDE[1, pl.ds(first + 1024, 256, stride=4), :] = dk[256:] * SCALE
                WIDE[2, pl.ds(first, 256, stride=4), :] = dv[:256] + dv_first
                WIDE[2, pl.ds(first + 1024, 256, stride=4), :] = dv[256:]
        return carry

    lax.fori_loop(0, 4, row_backward, 0)

    for copy in lx_in:
        copy.wait_recv()

    def finish(m, carry):
        rows = pl.ds(pl.multiple_of(m * 256, 256), 256)
        total = LR[3, rows, :].astype(F32) + LX[0, rows, :].astype(F32) + LX[1, rows, :].astype(F32)
        LX[0, rows, :] = total.astype(BF16)
        return carry

    lax.fori_loop(0, 4, finish, 0)
    copy = pltpu.make_async_copy(LX.at[0], lay_out, loc.at[11])
    copy.start()
    stores.append(copy)

    for q in range(4):
        reduce_end(q)

    for t, dst in enumerate((dq_out, dk_out, dv_out)):
        for copy in dg_in[15 * t : 15 * t + 15]:
            copy.wait_recv()

        def spread(m, carry, t=t):
            for hh in range(2):
                block = RDG[t, pl.ds(m * 4, 4), hh].astype(F32)
                for r in range(2):
                    first = r * 2048 + 2 * hh + 1 + m * 512
                    WIDE[t, pl.ds(first, 128, stride=4), :] = block[:, :, 8 * r : 8 * r + 8, :].reshape(128, 128)
            return carry

        lax.fori_loop(0, 4, spread, 0)

        def narrow(m, carry, t=t):
            rows = pl.ds(pl.multiple_of(m * 512, 512), 512)
            RAW[t, rows, :] = WIDE[t, rows, :].astype(BF16)
            return carry

        lax.fori_loop(0, 8, narrow, 0)
        copy = pltpu.make_async_copy(RAW.at[t], dst, loc.at[8 + t])
        copy.start()
        stores.append(copy)
    for copy in stores:
        copy.wait()
    for copy in sends:
        copy.wait_send()


def on_device(queries, keys, values, out_grad, wo):
    flat = tuple(t.reshape(4096, 128) for t in (queries, keys, values))
    flat_shape = jax.ShapeDtypeStruct((4096, 128), BF16)
    any_spec = pl.BlockSpec(memory_space=pl.ANY)

    def vmem(*shape, dtype=BF16):
        return pltpu.VMEM(shape, dtype)

    def sems(*shape):
        return pltpu.SemaphoreType.DMA(shape)

    out = pl.pallas_call(
        kernel,
        name="layer",
        out_shape=(
            jax.ShapeDtypeStruct((1024, 512), BF16),
            flat_shape, flat_shape, flat_shape,
            jax.ShapeDtypeStruct((512, 256), BF16),
        ),
        in_specs=[any_spec] * 5,
        out_specs=[any_spec] * 5,
        scratch_shapes=[
            vmem(3, 4096, 128),
            vmem(3, 4096, 128, dtype=F32),
            vmem(3, 16, 2, 4, 16, 128),
            vmem(3, 16, 2, 4, 16, 128),
            vmem(512, 4096),
            vmem(1024, 4096),
            vmem(3, 4, 512, 128),
            vmem(3, 16, 2, 4, 16, 128),
            vmem(16, 2, 4, 16, 128),
            vmem(16, 2, 4, 16, 128),
            vmem(16, 2, 4, 16, 128),
            vmem(16, 2, 4, 16, 128),
            vmem(3, 16, 2, 4, 16, 128),
            vmem(8, 256, 256, dtype=F32),
            vmem(4, 512, 512, dtype=F32),
            vmem(1024, 512),
            vmem(512, 1024),
            vmem(2, 16, 4, 8, 256, dtype=F32),
            vmem(1024, 256),
            vmem(4, 4, 4, 128, 256),
            vmem(4, 2, 2, 128, 256),
            vmem(4, 2, 4, 128, 256),
            vmem(4, 4, 128, 256),
            vmem(4, 3, 128, 256),
            vmem(4, 1024, 512),
            vmem(4, 1024, 512),
            vmem(2, 1024, 512),
            vmem(2, 512, 512),
            vmem(4, 128, 256),
            sems(16),
            sems(3, 15), sems(3, 15),
            sems(15), sems(15),
            sems(15), sems(15),
            sems(3, 15), sems(3, 15),
            sems(6), sems(6),
            sems(3, 2), sems(3, 2),
            sems(3, 2), sems(3, 2),
            sems(2, 3, 2), sems(2, 3, 2),
            sems(4, 6), sems(4, 6),
            sems(4, 3), sems(4, 3),
            sems(4), sems(4),
            sems(6), sems(6),
        ],
        compiler_params=pltpu.CompilerParams(
            collective_id=0, has_side_effects=True, vmem_limit_bytes=63 << 20
        ),
    )(*flat, out_grad, wo)
    lay, dq, dk, dv, pg = out
    return lay, *(t.reshape(1024, 4, 128) for t in (dq, dk, dv)), pg


def solution(mesh):
    in_specs = (
        P("ctx", "head", None),
        P("ctx", "head", None),
        P("ctx", "head", None),
        P("ctx", None),
        P("head", "ctx"),
    )
    out_specs = (
        P("ctx", "head"),
        P("ctx", "head", None),
        P("ctx", "head", None),
        P("ctx", "head", None),
        P("head", "ctx"),
    )
    return jax.shard_map(
        on_device, mesh=mesh, in_specs=in_specs, out_specs=out_specs, check_vma=False
    )
```

```python
import jax
import jax.numpy as jnp
from jax import lax
from jax.experimental import pallas as pl
from jax.experimental.pallas import tpu as pltpu
from jax.sharding import PartitionSpec as P

MESH = pl.DeviceIdType.MESH
BF16 = jnp.bfloat16
F32 = jnp.float32
SCALE = 128 ** -0.5
SEVEN = tuple((dy, dz) for dy in range(4) for dz in range(4) if dy or dz)


def nt(a, b):
    return lax.dot_general(a, b, (((1,), (1,)), ((), ())), preferred_element_type=F32)


def nn(a, b):
    return lax.dot_general(a, b, (((1,), (0,)), ((), ())), preferred_element_type=F32)


def tn(a, b):
    return lax.dot_general(a, b, (((0,), (0,)), ((), ())), preferred_element_type=F32)


def softmax(scores, visible):
    scores = jnp.where(visible, scores * SCALE, -jnp.inf)
    lifted = jnp.exp(scores - jnp.max(scores, axis=-1, keepdims=True))
    return lifted / jnp.sum(lifted, axis=-1, keepdims=True)


def score_gradient(p, dp):
    return (p * (dp - jnp.sum(p * dp, axis=-1, keepdims=True))).astype(BF16)


def kernel(
    q_hbm, k_hbm, v_hbm, og_hbm, wo_hbm,
    lay_out, dq_out, dk_out, dv_out, pg_out,
    WIDE, QS, RDG,
    W, OG, QKVR, REC, RDO, SO, RO, PC, PR, ATT, ATTT, AGF, AGR, PP, RL, R1, S2, R2, LS, LR, LX, XR,
    loc, qkv_s, qkv_r, o_s, o_r, do_s, do_r, dg_s, dg_r, w1_s, w1_r, wa_s, wa_r, wb_s, wb_r, wc_s, wc_r,
    p1_s, p1_r, p2_s, p2_r, lp_s, lp_r, lx_s, lx_r,
):
    c = lax.axis_index("ctx")
    h = lax.axis_index("head")
    y, z = c // 4, lax.rem(c, 4)
    x, core = h // 2, lax.rem(h, 2)

    def grid_peer(dy, dz):
        return lax.rem(y + dy, 4) * 4 + lax.rem(z + dz, 4)

    def x_head(dx):
        return lax.rem(x + dx, 4) * 2 + core

    partner = (c, x * 2 + (1 - core))

    def remote(src, dst, ssem, rsem, dev):
        return pltpu.make_async_remote_copy(
            src_ref=src, dst_ref=dst, send_sem=ssem, recv_sem=rsem, device_id=dev, device_id_type=MESH
        )

    sends = []

    def push(copy):
        copy.start()
        sends.append(copy)
        return copy

    def drain(copies):
        for copy in copies:
            copy.wait_send()
            sends[:] = [other for other in sends if other is not copy]

    flat_out = (dq_out, dk_out, dv_out)
    own_cols = pl.ds(pl.multiple_of(c * 256, 256), 256)

    loads_q = []
    for t, src in enumerate((q_hbm, k_hbm, v_hbm)):
        copy = pltpu.make_async_copy(src, flat_out[t], loc.at[t])
        copy.start()
        loads_q.append(copy)
    loads_w = []
    for slot, j in enumerate((0, 2, 1, 3)):
        copy = pltpu.make_async_copy(
            wo_hbm.at[pl.ds(j * 128, 128)], W.at[pl.ds(slot * 128, 128), own_cols], loc.at[3 + slot]
        )
        copy.start()
        loads_w.append(copy)
    load_og = pltpu.make_async_copy(og_hbm, OG, loc.at[7])
    load_og.start()

    barrier = pltpu.get_barrier_semaphore()
    for dy, dz in SEVEN:
        pl.semaphore_signal(barrier, inc=1, device_id=(grid_peer(dy, dz), h), device_id_type=MESH)
    for dx in range(1, 4):
        pl.semaphore_signal(barrier, inc=1, device_id=(c, x_head(dx)), device_id_type=MESH)
    pl.semaphore_signal(barrier, inc=1, device_id=partner, device_id_type=MESH)

    def unpack(t):
        loads_q[t].wait()

        def widen(m, carry):
            rows = pl.ds(pl.multiple_of(m * 512, 512), 512)
            WIDE[t, rows, :] = flat_out[t][rows, :].astype(F32)
            return carry

        lax.fori_loop(0, 8, widen, 0)

        def strided(m, carry):
            for hh in range(2):
                both = []
                for r in range(2):
                    first = r * 2048 + 2 * hh + 1 + m * 512
                    both.append(WIDE[t, pl.ds(first, 128, stride=4), :].reshape(4, 4, 8, 128))
                QS[t, pl.ds(m * 4, 4), hh] = jnp.concatenate(both, axis=2).astype(BF16)
            return carry

        lax.fori_loop(0, 4, strided, 0)

    unpack(0)
    for copy in loads_w:
        copy.wait()
    pl.semaphore_wait(barrier, 19)

    w_own = W.at[:, own_cols]
    wz, wy = [], []
    for d in range(1, 4):
        wz.append(push(remote(w_own, w_own, w1_s.at[d - 1], w1_r.at[d - 1], (grid_peer(0, d), h))))
        wy.append(push(remote(w_own, w_own, w1_s.at[2 + d], w1_r.at[2 + d], (grid_peer(d, 0), h))))

    qkv_in = []

    def send_strided(t):
        for i, (dy, dz) in enumerate(SEVEN):
            to = grid_peer(dy, dz)
            qkv_in.append(push(remote(QS.at[t, to], REC.at[t, c], qkv_s.at[t, i], qkv_r.at[t, i], (to, h))))
        REC[t, c] = QS[t, c]

    send_strided(0)
    unpack(1)
    send_strided(1)
    unpack(2)
    send_strided(2)

    def w_block(first, size, owner):
        return W.at[pl.ds(first, size), pl.ds(pl.multiple_of(owner * 256, 256), 256)]

    wa = [[None] * 2 for _ in range(3)]
    wb = [[None] * 2 for _ in range(3)]

    def spread_w():
        for d in range(1, 4):
            wz[d - 1].wait_recv()
            block = w_block(0, 256, grid_peer(0, 4 - d))
            for k, e in enumerate((1, 3)):
                wa[d - 1][k] = push(
                    remote(block, block, wa_s.at[d - 1, k], wa_r.at[d - 1, k], (grid_peer(e, 0), h))
                )
            wy[d - 1].wait_recv()
            block = w_block(256, 256, grid_peer(4 - d, 0))
            for k, e in enumerate((1, 3)):
                wb[d - 1][k] = push(
                    remote(block, block, wb_s.at[d - 1, k], wb_r.at[d - 1, k], (grid_peer(0, e), h))
                )

    wc = []

    def relay_w():
        for d in range(1, 4):
            for k, e in enumerate((1, 3)):
                wa[d - 1][k].wait_recv()
                block = w_block(128 * k, 128, grid_peer(4 - e, 4 - d))
                wc.append(push(remote(block, block, wc_s.at[0, d - 1, k], wc_r.at[0, d - 1, k], (grid_peer(e, 0), h))))
                wb[d - 1][k].wait_recv()
                block = w_block(256 + 128 * k, 128, grid_peer(4 - d, 4 - e))
                wc.append(push(remote(block, block, wc_s.at[1, d - 1, k], wc_r.at[1, d - 1, k], (grid_peer(0, e), h))))

    def unpack_rows(m, carry):
        for t in range(3):
            for hh in range(2):
                rows = WIDE[t, pl.ds(m * 512 + 2 * hh, 128, stride=4), :].astype(BF16)
                QKVR[t, (m // 4) * 2 + hh, pl.ds(pl.multiple_of(lax.rem(m, 4) * 128, 128), 128), :] = rows
        return carry

    lax.fori_loop(0, 8, unpack_rows, 0)

    def causal(rows, cols, first):
        return (
            lax.broadcasted_iota(jnp.int32, (rows, cols), 0) + first
            >= lax.broadcasted_iota(jnp.int32, (rows, cols), 1)
        )

    def row_forward(i, carry):
        r, hh = i // 2, lax.rem(i, 2)
        lanes = pl.ds(pl.multiple_of(hh * 128, 128), 128)
        for b in range(2):
            n = 256 * (b + 1)
            q = QKVR[0, i, pl.ds(256 * b, 256), :]
            p = softmax(nt(q, QKVR[1, i, pl.ds(0, n), :]), causal(256, n, 256 * b))
            PR[i, pl.ds(256 * b, 256), pl.ds(0, n)] = p
            o = nn(p.astype(BF16), QKVR[2, i, pl.ds(0, n), :])
            rows = pl.ds(pl.multiple_of(r * 512 + 256 * b, 256), 256)
            ATT[rows, lanes] = o.astype(BF16)
            ATTT[lanes, rows] = o.T.astype(BF16)
        return carry

    lax.fori_loop(0, 4, row_forward, 0)

    def projection(half):
        def one(n, carry):
            cols = pl.ds(pl.multiple_of(n * 256, 256), 256)
            part = nn(ATTT[pl.ds(256 * half, 256), :], OG[:, cols])
            for q in range(2):
                PP[2 * half + q, n // 4, lax.rem(n, 4)] = part[128 * q : 128 * q + 128].astype(BF16)
            return carry

        lax.fori_loop(0, 16, one, 0)

    spread_w()
    load_og.wait()
    projection(0)

    first_half, second_half = pl.ds(0, 2), pl.ds(2, 2)

    def group(q, d, part):
        if q % 2 == 0:
            return PP.at[q, part, lax.rem(z + d, 4)]
        return PP.at[q, lax.rem(y + d, 4), part]

    def along(q, d, second=False):
        return (grid_peer(0, d) if (q % 2 == 0) != second else grid_peer(d, 0), h)

    pr_in, p1_in, p2_in = [None] * 4, [None] * 4, [None] * 4

    def reduce_start(q):
        pr_in[q] = [
            push(remote(group(q, 2, first_half), RL.at[q, 0], p1_s.at[q, 0], p1_r.at[q, 0], along(q, 1))),
            push(remote(group(q, 2, second_half), RL.at[q, 1], p1_s.at[q, 1], p1_r.at[q, 1], along(q, 3))),
        ]
        p1_in[q] = [
            push(remote(group(q, 1, second_half), R1.at[q, 0, second_half], p1_s.at[q, 2], p1_r.at[q, 2], along(q, 1))),
            push(remote(group(q, 3, first_half), R1.at[q, 1, first_half], p1_s.at[q, 3], p1_r.at[q, 3], along(q, 3))),
        ]

    def reduce_pass(q):
        for k, (d, part) in enumerate(((1, first_half), (3, second_half))):
            pr_in[q][k].wait_recv()
            mine = group(q, d, part)
            mine[...] = (mine[...].astype(F32) + RL[q, k].astype(F32)).astype(BF16)
            p1_in[q].append(
                push(remote(mine, R1.at[q, k, part], p1_s.at[q, 4 + k], p1_r.at[q, 4 + k], along(q, d)))
            )

    def reduce_middle(q):
        for copy in p1_in[q]:
            copy.wait_recv()
        p2_in[q] = []
        for d in (2, 1, 3, 0):
            if q % 2 == 0:
                other = lax.rem(y + d, 4)
                mine = PP[q, other, z]
            else:
                other = lax.rem(z + d, 4)
                mine = PP[q, y, other]
            total = mine.astype(F32) + R1[q, 0, other].astype(F32) + R1[q, 1, other].astype(F32)
            S2[q, d] = total.astype(BF16)
            if d:
                p2_in[q].append(
                    push(remote(S2.at[q, d], R2.at[q, d - 1], p2_s.at[q, d - 1], p2_r.at[q, d - 1], along(q, d, True)))
                )

    def reduce_end(q):
        for copy in p2_in[q]:
            copy.wait_recv()
        total = S2[q, 0].astype(F32)
        for k in range(3):
            total = total + R2[q, k].astype(F32)
        pg_out[pl.ds((2 * (q % 2) + q // 2) * 128, 128), :] = total.astype(BF16)

    for copy in qkv_in:
        copy.wait_recv()
    ii = lax.broadcasted_iota(jnp.int32, (256, 256), 0)
    jj = lax.broadcasted_iota(jnp.int32, (256, 256), 1)

    def tile(ref):
        return ref.reshape(256, 128)

    def col_forward(i, carry):
        hh, g = i // 4, lax.rem(i, 4)
        visible = (lax.rem(ii, 8) == lax.rem(jj, 8)) & (ii >= jj)
        p = softmax(nt(tile(REC[0, :, hh, g]), tile(REC[1, :, hh, g])), visible)
        PC[i] = p
        o = nn(p.astype(BF16), tile(REC[2, :, hh, g]))
        SO[:, hh, g] = o.astype(BF16).reshape(16, 16, 128)
        return carry

    lax.fori_loop(0, 8, col_forward, 0, unroll=2)
    o_in = []
    for i, (dy, dz) in enumerate(SEVEN):
        to = grid_peer(dy, dz)
        o_in.append(push(remote(SO.at[to], RO.at[c], o_s.at[i], o_r.at[i], (to, h))))
    RO[c] = SO[c]

    relay_w()
    reduce_start(0)
    reduce_start(1)

    for copy in o_in:
        copy.wait_recv()
    for hh in range(2):
        for g in range(4):
            block = RO[:, hh, g].astype(F32)
            for r in range(2):
                AGF[r, :, g, :, pl.ds(hh * 128, 128)] = block[:, 8 * r : 8 * r + 8, :]

    def place(m, carry):
        block = AGF[m // 2, pl.ds(pl.multiple_of(lax.rem(m, 2) * 8, 8), 8)].reshape(256, 256)
        rows = pl.ds(pl.multiple_of(m * 256, 256), 256)
        ATT[rows, pl.ds(256, 256)] = block.astype(BF16)
        ATTT[pl.ds(256, 256), rows] = block.T.astype(BF16)
        return carry

    lax.fori_loop(0, 4, place, 0)
    projection(1)

    for copy in wc:
        copy.wait_recv()

    def strided_cotangent(m, carry):
        rows = pl.ds(pl.multiple_of(m * 256, 256), 256)
        part = nt(OG[rows, :], W[pl.ds(256, 256), :])
        AGF[m // 2, pl.ds(pl.multiple_of(lax.rem(m, 2) * 8, 8), 8)] = part.reshape(8, 4, 8, 256)
        return carry

    lax.fori_loop(0, 4, strided_cotangent, 0)
    drain(o_in)
    for hh in range(2):
        for g in range(4):
            lanes = pl.ds(hh * 128, 128)
            both = jnp.concatenate([AGF[0, :, g, :, lanes], AGF[1, :, g, :, lanes]], axis=1)
            SO[:, hh, g] = both.astype(BF16)
    do_in = []
    for i, (dy, dz) in enumerate(SEVEN):
        to = grid_peer(dy, dz)
        do_in.append(push(remote(SO.at[to], RDO.at[c], do_s.at[i], do_r.at[i], (to, h))))
    RDO[c] = SO[c]
    reduce_start(2)
    reduce_start(3)
    reduce_pass(0)
    reduce_pass(1)

    def partial_out(m, head):
        rows = pl.ds(pl.multiple_of(m * 256, 256), 256)
        cols = pl.ds(pl.multiple_of(head * 512, 512), 512)
        return rows, nn(ATT[rows, :], W[:, cols])

    order = (2, 1, 3, 0)
    lp_in = [None] * 4

    def to_partner(n):
        head = lax.rem(x + order[n], 4) * 2 + (1 - core)

        def for_partner(m, carry):
            rows, part = partial_out(m, head)
            LS[n, rows, :] = part.astype(BF16)
            return carry

        lax.fori_loop(0, 4, for_partner, 0)
        lp_in[n] = push(remote(LS.at[n], LR.at[n], lp_s.at[n], lp_r.at[n], partner))

    def to_x(n):
        head = x_head(order[n])
        lp_in[n].wait_recv()

        def for_x(m, carry):
            rows, part = partial_out(m, head)
            LR[n, rows, :] = (part + LR[n, rows, :].astype(F32)).astype(BF16)
            return carry

        lax.fori_loop(0, 4, for_x, 0)

    lower, upper = pl.ds(0, 512), pl.ds(512, 512)
    ahead, behind = (c, x_head(1)), (c, x_head(3))

    def add_passing(n, k, rows):
        relay[k].wait_recv()
        LR[n, rows, :] = (LR[n, rows, :].astype(F32) + XR[k].astype(F32)).astype(BF16)

    to_partner(0)
    to_partner(1)
    to_x(0)
    relay = [
        push(remote(LR.at[0, lower], XR.at[0], lx_s.at[0], lx_r.at[0], ahead)),
        push(remote(LR.at[0, upper], XR.at[1], lx_s.at[1], lx_r.at[1], behind)),
    ]
    to_partner(2)
    to_x(1)
    lx_in = [push(remote(LR.at[1, upper], LX.at[0, upper], lx_s.at[2], lx_r.at[2], ahead))]
    to_partner(3)
    to_x(2)
    lx_in.append(push(remote(LR.at[2, lower], LX.at[1, lower], lx_s.at[3], lx_r.at[3], behind)))

    for copy in do_in:
        copy.wait_recv()

    def col_backward(i, carry):
        hh, g = i // 4, lax.rem(i, 4)
        p = PC[i]
        grad = tile(RDO[:, hh, g])
        low = score_gradient(p, nt(grad, tile(REC[2, :, hh, g])))
        QS[0, :, hh, g] = (nn(low, tile(REC[1, :, hh, g])) * SCALE).astype(BF16).reshape(16, 16, 128)
        QS[1, :, hh, g] = (tn(low, tile(REC[0, :, hh, g])) * SCALE).astype(BF16).reshape(16, 16, 128)
        QS[2, :, hh, g] = tn(p.astype(BF16), grad).astype(BF16).reshape(16, 16, 128)
        return carry

    drain(qkv_in)
    lax.fori_loop(0, 8, col_backward, 0, unroll=2)
    reduce_pass(2)
    reduce_pass(3)
    dg_in = []
    for t in range(3):
        for i, (dy, dz) in enumerate(SEVEN):
            to = grid_peer(dy, dz)
            dg_in.append(push(remote(QS.at[t, to], RDG.at[t, c], dg_s.at[t, i], dg_r.at[t, i], (to, h))))
        RDG[t, c] = QS[t, c]

    to_x(3)
    add_passing(1, 0, lower)
    lx_in.append(push(remote(LR.at[1, lower], LX.at[0, lower], lx_s.at[4], lx_r.at[4], ahead)))
    add_passing(2, 1, upper)
    lx_in.append(push(remote(LR.at[2, upper], LX.at[1, upper], lx_s.at[5], lx_r.at[5], behind)))

    reduce_middle(0)
    reduce_middle(1)
    reduce_middle(2)
    reduce_middle(3)

    def row_cotangent(m, carry):
        rows = pl.ds(pl.multiple_of(m * 256, 256), 256)
        AGR[rows, :] = nt(OG[rows, :], W[pl.ds(0, 256), :]).astype(BF16)
        return carry

    lax.fori_loop(0, 4, row_cotangent, 0)

    def row_backward(i, carry):
        r, hh = i // 2, lax.rem(i, 2)
        lanes = pl.ds(pl.multiple_of(hh * 128, 128), 128)
        for b in range(2):
            n = 256 * (b + 1)
            rows = pl.ds(256 * b, 256)
            seen = pl.ds(0, n)
            p = PR[i, rows, seen]
            grad = AGR[pl.ds(pl.multiple_of(r * 512 + 256 * b, 256), 256), lanes]
            low = score_gradient(p, nt(grad, QKVR[2, i, seen, :]))
            first = r * 2048 + 2 * hh
            WIDE[0, pl.ds(first + 1024 * b, 256, stride=4), :] = nn(low, QKVR[1, i, seen, :]) * SCALE
            dk = tn(low, QKVR[0, i, rows, :])
            dv = tn(p.astype(BF16), grad)
            if b == 0:
                dk_first, dv_first = dk, dv
            else:
                WIDE[1, pl.ds(first, 256, stride=4), :] = (dk[:256] + dk_first) * SCALE
                WIDE[1, pl.ds(first + 1024, 256, stride=4), :] = dk[256:] * SCALE
                WIDE[2, pl.ds(first, 256, stride=4), :] = dv[:256] + dv_first
                WIDE[2, pl.ds(first + 1024, 256, stride=4), :] = dv[256:]
        return carry

    lax.fori_loop(0, 4, row_backward, 0)

    for q in range(4):
        reduce_end(q)

    for t in range(3):
        for copy in dg_in[15 * t : 15 * t + 15]:
            copy.wait_recv()

        def spread(m, carry, t=t):
            for hh in range(2):
                block = RDG[t, pl.ds(m * 4, 4), hh].astype(F32)
                for r in range(2):
                    first = r * 2048 + 2 * hh + 1 + m * 512
                    WIDE[t, pl.ds(first, 128, stride=4), :] = block[:, :, 8 * r : 8 * r + 8, :].reshape(128, 128)
            return carry

        lax.fori_loop(0, 4, spread, 0)

        def narrow(m, carry, t=t):
            rows = pl.ds(pl.multiple_of(m * 512, 512), 512)
            flat_out[t][rows, :] = WIDE[t, rows, :].astype(BF16)
            return carry

        lax.fori_loop(0, 8, narrow, 0)
    for copy in lx_in:
        copy.wait_recv()

    def finish(m, carry):
        rows = pl.ds(pl.multiple_of(m * 256, 256), 256)
        total = LR[3, rows, :].astype(F32) + LX[0, rows, :].astype(F32) + LX[1, rows, :].astype(F32)
        lay_out[rows, :] = total.astype(BF16)
        return carry

    lax.fori_loop(0, 4, finish, 0)
    for copy in sends:
        copy.wait_send()


def store(*refs):
    done = refs[10]
    copies = [pltpu.make_async_copy(refs[i], refs[5 + i], done.at[i]) for i in range(5)]
    for copy in copies:
        copy.start()
    for copy in copies:
        copy.wait()


def on_device(queries, keys, values, out_grad, wo):
    flat = tuple(t.reshape(4096, 128) for t in (queries, keys, values))
    flat_shape = pltpu.VMEM((4096, 128), BF16)
    any_spec = pl.BlockSpec(memory_space=pl.ANY)

    def vmem(*shape, dtype=BF16):
        return pltpu.VMEM(shape, dtype)

    def sems(*shape):
        return pltpu.SemaphoreType.DMA(shape)

    out = pl.pallas_call(
        kernel,
        name="layer",
        out_shape=(
            pltpu.VMEM((1024, 512), BF16),
            flat_shape, flat_shape, flat_shape,
            pltpu.VMEM((512, 256), BF16),
        ),
        in_specs=[any_spec] * 5,
        out_specs=[pl.BlockSpec(memory_space=pltpu.VMEM)] * 5,
        scratch_shapes=[
            vmem(3, 4096, 128, dtype=F32),
            vmem(3, 16, 2, 4, 16, 128),
            vmem(3, 16, 2, 4, 16, 128),
            vmem(512, 4096),
            vmem(1024, 4096),
            vmem(3, 4, 512, 128),
            vmem(3, 16, 2, 4, 16, 128),
            vmem(16, 2, 4, 16, 128),
            vmem(16, 2, 4, 16, 128),
            vmem(16, 2, 4, 16, 128),
            vmem(8, 256, 256, dtype=F32),
            vmem(4, 512, 512, dtype=F32),
            vmem(1024, 512),
            vmem(512, 1024),
            vmem(2, 16, 4, 8, 256, dtype=F32),
            vmem(1024, 256),
            vmem(4, 4, 4, 128, 256),
            vmem(4, 2, 2, 128, 256),
            vmem(4, 2, 4, 128, 256),
            vmem(4, 4, 128, 256),
            vmem(4, 3, 128, 256),
            vmem(4, 1024, 512),
            vmem(4, 1024, 512),
            vmem(2, 1024, 512),
            vmem(2, 512, 512),
            sems(8),
            sems(3, 15), sems(3, 15),
            sems(15), sems(15),
            sems(15), sems(15),
            sems(3, 15), sems(3, 15),
            sems(6), sems(6),
            sems(3, 2), sems(3, 2),
            sems(3, 2), sems(3, 2),
            sems(2, 3, 2), sems(2, 3, 2),
            sems(4, 6), sems(4, 6),
            sems(4, 3), sems(4, 3),
            sems(4), sems(4),
            sems(6), sems(6),
        ],
        compiler_params=pltpu.CompilerParams(
            collective_id=0, has_side_effects=True, vmem_limit_bytes=58 << 20
        ),
    )(*flat, out_grad, wo)
    lay, dq, dk, dv, pg = pl.pallas_call(
        store,
        name="store",
        out_shape=tuple(jax.ShapeDtypeStruct(t.shape, t.dtype) for t in out),
        in_specs=[any_spec] * 5,
        out_specs=[any_spec] * 5,
        scratch_shapes=[sems(5)],
        compiler_params=pltpu.CompilerParams(vmem_limit_bytes=1 << 20),
    )(*out)
    return lay, *(t.reshape(1024, 4, 128) for t in (dq, dk, dv)), pg


def solution(mesh):
    in_specs = (
        P("ctx", "head", None),
        P("ctx", "head", None),
        P("ctx", "head", None),
        P("ctx", None),
        P("head", "ctx"),
    )
    out_specs = (
        P("ctx", "head"),
        P("ctx", "head", None),
        P("ctx", "head", None),
        P("ctx", "head", None),
        P("head", "ctx"),
    )
    return jax.shard_map(
        on_device, mesh=mesh, in_specs=in_specs, out_specs=out_specs, check_vma=False
    )
```

```python
import jax
import jax.numpy as jnp
from jax import lax
from jax.experimental import pallas as pl
from jax.experimental.pallas import tpu as pltpu
from jax.sharding import PartitionSpec as P

MESH = pl.DeviceIdType.MESH
BF16 = jnp.bfloat16
F32 = jnp.float32
SCALE = 128 ** -0.5
SEVEN = tuple((dy, dz) for dy in range(4) for dz in range(4) if dy or dz)


def nt(a, b):
    return lax.dot_general(a, b, (((1,), (1,)), ((), ())), preferred_element_type=F32)


def nn(a, b):
    return lax.dot_general(a, b, (((1,), (0,)), ((), ())), preferred_element_type=F32)


def tn(a, b):
    return lax.dot_general(a, b, (((0,), (0,)), ((), ())), preferred_element_type=F32)


def softmax(scores, visible):
    scores = jnp.where(visible, scores * SCALE, -jnp.inf)
    lifted = jnp.exp(scores - jnp.max(scores, axis=-1, keepdims=True))
    return lifted / jnp.sum(lifted, axis=-1, keepdims=True)


def score_gradient(p, dp):
    return (p * (dp - jnp.sum(p * dp, axis=-1, keepdims=True))).astype(BF16)


def kernel(
    q_hbm, k_hbm, v_hbm, og_hbm, wo_hbm,
    lay_out, dq_out, dk_out, dv_out, pg_out,
    WIDE, QS, RDG,
    W, OG, QKVR, REC, RDO, SO, RO, PC, PR, ATT, ATTT, AGF, AGR, PP, RL, R1, S2, R2, LS, LR, LX, XR,
    loc, qkv_s, qkv_r, o_s, o_r, do_s, do_r, dg_s, dg_r, w1_s, w1_r, wa_s, wa_r, wb_s, wb_r, wc_s, wc_r,
    p1_s, p1_r, p2_s, p2_r, lp_s, lp_r, lx_s, lx_r,
):
    c = lax.axis_index("ctx")
    h = lax.axis_index("head")
    y, z = c // 4, lax.rem(c, 4)
    x, core = h // 2, lax.rem(h, 2)

    def grid_peer(dy, dz):
        return lax.rem(y + dy, 4) * 4 + lax.rem(z + dz, 4)

    def x_head(dx):
        return lax.rem(x + dx, 4) * 2 + core

    partner = (c, x * 2 + (1 - core))

    def remote(src, dst, ssem, rsem, dev):
        return pltpu.make_async_remote_copy(
            src_ref=src, dst_ref=dst, send_sem=ssem, recv_sem=rsem, device_id=dev, device_id_type=MESH
        )

    sends = []

    def push(copy):
        copy.start()
        sends.append(copy)
        return copy

    def drain(copies):
        for copy in copies:
            copy.wait_send()
            sends[:] = [other for other in sends if other is not copy]

    flat_out = (dq_out, dk_out, dv_out)
    own_cols = pl.ds(pl.multiple_of(c * 256, 256), 256)

    loads_q = []
    for t, src in enumerate((q_hbm, k_hbm, v_hbm)):
        copy = pltpu.make_async_copy(src, flat_out[t], loc.at[t])
        copy.start()
        loads_q.append(copy)
    loads_w = []
    for slot, j in enumerate((0, 2, 1, 3)):
        copy = pltpu.make_async_copy(
            wo_hbm.at[pl.ds(j * 128, 128)], W.at[pl.ds(slot * 128, 128), own_cols], loc.at[3 + slot]
        )
        copy.start()
        loads_w.append(copy)
    load_og = pltpu.make_async_copy(og_hbm, OG, loc.at[7])
    load_og.start()

    barrier = pltpu.get_barrier_semaphore()
    for dy, dz in SEVEN:
        pl.semaphore_signal(barrier, inc=1, device_id=(grid_peer(dy, dz), h), device_id_type=MESH)
    for dx in range(1, 4):
        pl.semaphore_signal(barrier, inc=1, device_id=(c, x_head(dx)), device_id_type=MESH)
    pl.semaphore_signal(barrier, inc=1, device_id=partner, device_id_type=MESH)

    def unpack(t):
        loads_q[t].wait()

        def widen(m, carry):
            rows = pl.ds(pl.multiple_of(m * 512, 512), 512)
            WIDE[t, rows, :] = flat_out[t][rows, :].astype(F32)
            return carry

        lax.fori_loop(0, 8, widen, 0)

        def strided(m, carry):
            for hh in range(2):
                both = []
                for r in range(2):
                    first = r * 2048 + 2 * hh + 1 + m * 512
                    both.append(WIDE[t, pl.ds(first, 128, stride=4), :].reshape(4, 4, 8, 128))
                QS[t, pl.ds(m * 4, 4), hh] = jnp.concatenate(both, axis=2).astype(BF16)
            return carry

        lax.fori_loop(0, 4, strided, 0)

    unpack(0)
    for copy in loads_w:
        copy.wait()
    pl.semaphore_wait(barrier, 19)

    w_own = W.at[:, own_cols]
    wz, wy = {}, {}
    for k, d in enumerate((1, 3)):
        wz[d] = push(remote(w_own, w_own, w1_s.at[k], w1_r.at[k], (grid_peer(0, d), h)))
        wy[d] = push(remote(w_own, w_own, w1_s.at[2 + k], w1_r.at[2 + k], (grid_peer(d, 0), h)))

    qkv_in = []

    def send_strided(t):
        for i, (dy, dz) in enumerate(SEVEN):
            to = grid_peer(dy, dz)
            qkv_in.append(push(remote(QS.at[t, to], REC.at[t, c], qkv_s.at[t, i], qkv_r.at[t, i], (to, h))))
        REC[t, c] = QS[t, c]

    send_strided(0)
    unpack(1)
    send_strided(1)
    unpack(2)
    send_strided(2)

    def w_block(first, size, owner):
        return W.at[pl.ds(first, size), pl.ds(pl.multiple_of(owner * 256, 256), 256)]

    wa = [[None] * 2 for _ in range(3)]
    wb = [[None] * 2 for _ in range(3)]
    wr = []

    def spread_along(d):
        block = w_block(0, 256, grid_peer(0, 4 - d))
        for k, e in enumerate((1, 3)):
            wa[d - 1][k] = push(remote(block, block, wa_s.at[d - 1, k], wa_r.at[d - 1, k], (grid_peer(e, 0), h)))
        block = w_block(256, 256, grid_peer(4 - d, 0))
        for k, e in enumerate((1, 3)):
            wb[d - 1][k] = push(remote(block, block, wb_s.at[d - 1, k], wb_r.at[d - 1, k], (grid_peer(0, e), h)))

    def spread_w():
        for d in (1, 3):
            wz[d].wait_recv()
            wy[d].wait_recv()
        for k, (first, dy, dz) in enumerate(((0, 0, 1), (256, 0, 3), (256, 1, 0), (0, 3, 0))):
            block = w_block(first, 256, grid_peer((4 - dy) % 4, (4 - dz) % 4))
            wr.append(push(remote(block, block, w1_s.at[4 + k], w1_r.at[4 + k], (grid_peer(dy, dz), h))))
        spread_along(1)
        spread_along(3)

    def spread_far():
        for copy in wr:
            copy.wait_recv()
        spread_along(2)

    wc = []

    def relay_w(d):
        for k, e in enumerate((1, 3)):
            wa[d - 1][k].wait_recv()
            block = w_block(128 * k, 128, grid_peer(4 - e, 4 - d))
            wc.append(push(remote(block, block, wc_s.at[0, d - 1, k], wc_r.at[0, d - 1, k], (grid_peer(e, 0), h))))
            wb[d - 1][k].wait_recv()
            block = w_block(256 + 128 * k, 128, grid_peer(4 - d, 4 - e))
            wc.append(push(remote(block, block, wc_s.at[1, d - 1, k], wc_r.at[1, d - 1, k], (grid_peer(0, e), h))))

    def unpack_rows(m, carry):
        for t in range(3):
            for hh in range(2):
                rows = WIDE[t, pl.ds(m * 512 + 2 * hh, 128, stride=4), :].astype(BF16)
                QKVR[t, (m // 4) * 2 + hh, pl.ds(pl.multiple_of(lax.rem(m, 4) * 128, 128), 128), :] = rows
        return carry

    lax.fori_loop(0, 8, unpack_rows, 0)

    def causal(rows, cols, first):
        return (
            lax.broadcasted_iota(jnp.int32, (rows, cols), 0) + first
            >= lax.broadcasted_iota(jnp.int32, (rows, cols), 1)
        )

    def row_forward(i, carry):
        r, hh = i // 2, lax.rem(i, 2)
        lanes = pl.ds(pl.multiple_of(hh * 128, 128), 128)
        for b in range(2):
            n = 256 * (b + 1)
            q = QKVR[0, i, pl.ds(256 * b, 256), :]
            p = softmax(nt(q, QKVR[1, i, pl.ds(0, n), :]), causal(256, n, 256 * b))
            PR[i, pl.ds(256 * b, 256), pl.ds(0, n)] = p
            o = nn(p.astype(BF16), QKVR[2, i, pl.ds(0, n), :])
            rows = pl.ds(pl.multiple_of(r * 512 + 256 * b, 256), 256)
            ATT[rows, lanes] = o.astype(BF16)
            ATTT[lanes, rows] = o.T.astype(BF16)
        return carry

    lax.fori_loop(0, 4, row_forward, 0)

    def projection(half):
        def one(n, carry):
            cols = pl.ds(pl.multiple_of(n * 256, 256), 256)
            part = nn(ATTT[pl.ds(256 * half, 256), :], OG[:, cols])
            for q in range(2):
                PP[2 * half + q, n // 4, lax.rem(n, 4)] = part[128 * q : 128 * q + 128].astype(BF16)
            return carry

        lax.fori_loop(0, 16, one, 0)

    spread_w()
    load_og.wait()
    projection(0)

    first_half, second_half = pl.ds(0, 2), pl.ds(2, 2)

    def group(q, d, part):
        if q % 2 == 0:
            return PP.at[q, part, lax.rem(z + d, 4)]
        return PP.at[q, lax.rem(y + d, 4), part]

    def along(q, d, second=False):
        return (grid_peer(0, d) if (q % 2 == 0) != second else grid_peer(d, 0), h)

    pr_in, p1_in, p2_in = [None] * 4, [None] * 4, [None] * 4

    def reduce_start(q):
        pr_in[q] = [
            push(remote(group(q, 2, first_half), RL.at[q, 0], p1_s.at[q, 0], p1_r.at[q, 0], along(q, 1))),
            push(remote(group(q, 2, second_half), RL.at[q, 1], p1_s.at[q, 1], p1_r.at[q, 1], along(q, 3))),
        ]
        p1_in[q] = [
            push(remote(group(q, 1, second_half), R1.at[q, 0, second_half], p1_s.at[q, 2], p1_r.at[q, 2], along(q, 1))),
            push(remote(group(q, 3, first_half), R1.at[q, 1, first_half], p1_s.at[q, 3], p1_r.at[q, 3], along(q, 3))),
        ]

    def reduce_pass(q):
        for k, (d, part) in enumerate(((1, first_half), (3, second_half))):
            pr_in[q][k].wait_recv()
            mine = group(q, d, part)
            mine[...] = (mine[...].astype(F32) + RL[q, k].astype(F32)).astype(BF16)
            p1_in[q].append(
                push(remote(mine, R1.at[q, k, part], p1_s.at[q, 4 + k], p1_r.at[q, 4 + k], along(q, d)))
            )

    def reduce_middle(q):
        for copy in p1_in[q]:
            copy.wait_recv()
        p2_in[q] = []
        for d in (2, 1, 3, 0):
            if q % 2 == 0:
                other = lax.rem(y + d, 4)
                mine = PP[q, other, z]
            else:
                other = lax.rem(z + d, 4)
                mine = PP[q, y, other]
            total = mine.astype(F32) + R1[q, 0, other].astype(F32) + R1[q, 1, other].astype(F32)
            S2[q, d] = total.astype(BF16)
            if d:
                p2_in[q].append(
                    push(remote(S2.at[q, d], R2.at[q, d - 1], p2_s.at[q, d - 1], p2_r.at[q, d - 1], along(q, d, True)))
                )

    def reduce_end(q):
        for copy in p2_in[q]:
            copy.wait_recv()
        total = S2[q, 0].astype(F32)
        for k in range(3):
            total = total + R2[q, k].astype(F32)
        pg_out[pl.ds((2 * (q % 2) + q // 2) * 128, 128), :] = total.astype(BF16)

    for copy in qkv_in:
        copy.wait_recv()
    ii = lax.broadcasted_iota(jnp.int32, (256, 256), 0)
    jj = lax.broadcasted_iota(jnp.int32, (256, 256), 1)

    def tile(ref):
        return ref.reshape(256, 128)

    def col_forward(i, carry):
        hh, g = i // 4, lax.rem(i, 4)
        visible = (lax.rem(ii, 8) == lax.rem(jj, 8)) & (ii >= jj)
        p = softmax(nt(tile(REC[0, :, hh, g]), tile(REC[1, :, hh, g])), visible)
        PC[i] = p
        o = nn(p.astype(BF16), tile(REC[2, :, hh, g]))
        SO[:, hh, g] = o.astype(BF16).reshape(16, 16, 128)
        return carry

    lax.fori_loop(0, 8, col_forward, 0, unroll=2)
    spread_far()
    o_in = []
    for i, (dy, dz) in enumerate(SEVEN):
        to = grid_peer(dy, dz)
        o_in.append(push(remote(SO.at[to], RO.at[c], o_s.at[i], o_r.at[i], (to, h))))
    RO[c] = SO[c]

    relay_w(1)
    relay_w(3)
    relay_w(2)
    reduce_start(0)
    reduce_start(1)

    for copy in o_in:
        copy.wait_recv()
    for hh in range(2):
        for g in range(4):
            block = RO[:, hh, g].astype(F32)
            for r in range(2):
                AGF[r, :, g, :, pl.ds(hh * 128, 128)] = block[:, 8 * r : 8 * r + 8, :]

    def place(m, carry):
        block = AGF[m // 2, pl.ds(pl.multiple_of(lax.rem(m, 2) * 8, 8), 8)].reshape(256, 256)
        rows = pl.ds(pl.multiple_of(m * 256, 256), 256)
        ATT[rows, pl.ds(256, 256)] = block.astype(BF16)
        ATTT[pl.ds(256, 256), rows] = block.T.astype(BF16)
        return carry

    lax.fori_loop(0, 4, place, 0)

    for copy in wc:
        copy.wait_recv()

    def partial_out(m, head):
        rows = pl.ds(pl.multiple_of(m * 256, 256), 256)
        cols = pl.ds(pl.multiple_of(head * 512, 512), 512)
        return rows, nn(ATT[rows, :], W[:, cols])

    order = (2, 1, 3, 0)
    lp_in = [None] * 4

    def to_partner(n):
        head = lax.rem(x + order[n], 4) * 2 + (1 - core)

        def for_partner(m, carry):
            rows, part = partial_out(m, head)
            LS[n, rows, :] = part.astype(BF16)
            return carry

        lax.fori_loop(0, 4, for_partner, 0)
        lp_in[n] = push(remote(LS.at[n], LR.at[n], lp_s.at[n], lp_r.at[n], partner))

    def to_x(n):
        head = x_head(order[n])
        lp_in[n].wait_recv()

        def for_x(m, carry):
            rows, part = partial_out(m, head)
            LR[n, rows, :] = (part + LR[n, rows, :].astype(F32)).astype(BF16)
            return carry

        lax.fori_loop(0, 4, for_x, 0)

    lower, upper = pl.ds(0, 512), pl.ds(512, 512)
    ahead, behind = (c, x_head(1)), (c, x_head(3))

    def add_passing(n, k, rows):
        relay[k].wait_recv()
        LR[n, rows, :] = (LR[n, rows, :].astype(F32) + XR[k].astype(F32)).astype(BF16)

    def add_x():
        add_passing(1, 0, lower)
        lx_in.append(push(remote(LR.at[1, lower], LX.at[0, lower], lx_s.at[4], lx_r.at[4], ahead)))
        add_passing(2, 1, upper)
        lx_in.append(push(remote(LR.at[2, upper], LX.at[1, upper], lx_s.at[5], lx_r.at[5], behind)))

    def strided_cotangent(m, carry):
        rows = pl.ds(pl.multiple_of(m * 256, 256), 256)
        part = nt(OG[rows, :], W[pl.ds(256, 256), :])
        AGF[m // 2, pl.ds(pl.multiple_of(lax.rem(m, 2) * 8, 8), 8)] = part.reshape(8, 4, 8, 256)
        return carry

    lax.fori_loop(0, 4, strided_cotangent, 0)
    drain(o_in)
    for hh in range(2):
        for g in range(4):
            lanes = pl.ds(hh * 128, 128)
            both = jnp.concatenate([AGF[0, :, g, :, lanes], AGF[1, :, g, :, lanes]], axis=1)
            SO[:, hh, g] = both.astype(BF16)
    do_in = []
    for i, (dy, dz) in enumerate(SEVEN):
        to = grid_peer(dy, dz)
        do_in.append(push(remote(SO.at[to], RDO.at[c], do_s.at[i], do_r.at[i], (to, h))))
    RDO[c] = SO[c]

    to_partner(0)
    to_partner(1)
    to_x(0)
    relay = [
        push(remote(LR.at[0, lower], XR.at[0], lx_s.at[0], lx_r.at[0], ahead)),
        push(remote(LR.at[0, upper], XR.at[1], lx_s.at[1], lx_r.at[1], behind)),
    ]
    reduce_pass(0)
    reduce_pass(1)
    projection(1)
    reduce_start(2)
    reduce_start(3)

    to_partner(2)
    to_x(1)
    lx_in = [push(remote(LR.at[1, upper], LX.at[0, upper], lx_s.at[2], lx_r.at[2], ahead))]
    to_partner(3)
    to_x(2)
    lx_in.append(push(remote(LR.at[2, lower], LX.at[1, lower], lx_s.at[3], lx_r.at[3], behind)))

    reduce_middle(0)
    reduce_middle(1)

    for copy in do_in:
        copy.wait_recv()

    def col_backward(i, carry):
        hh, g = i // 4, lax.rem(i, 4)
        p = PC[i]
        grad = tile(RDO[:, hh, g])
        low = score_gradient(p, nt(grad, tile(REC[2, :, hh, g])))
        QS[0, :, hh, g] = (nn(low, tile(REC[1, :, hh, g])) * SCALE).astype(BF16).reshape(16, 16, 128)
        QS[1, :, hh, g] = (tn(low, tile(REC[0, :, hh, g])) * SCALE).astype(BF16).reshape(16, 16, 128)
        QS[2, :, hh, g] = tn(p.astype(BF16), grad).astype(BF16).reshape(16, 16, 128)
        return carry

    drain(qkv_in)
    lax.fori_loop(0, 8, col_backward, 0, unroll=2)
    reduce_pass(2)
    reduce_pass(3)
    dg_in = []
    for t in range(3):
        for i, (dy, dz) in enumerate(SEVEN):
            to = grid_peer(dy, dz)
            dg_in.append(push(remote(QS.at[t, to], RDG.at[t, c], dg_s.at[t, i], dg_r.at[t, i], (to, h))))
        RDG[t, c] = QS[t, c]

    to_x(3)
    add_x()
    reduce_middle(2)
    reduce_middle(3)

    def row_cotangent(m, carry):
        rows = pl.ds(pl.multiple_of(m * 256, 256), 256)
        AGR[rows, :] = nt(OG[rows, :], W[pl.ds(0, 256), :]).astype(BF16)
        return carry

    lax.fori_loop(0, 4, row_cotangent, 0)

    def row_backward(i, carry):
        r, hh = i // 2, lax.rem(i, 2)
        lanes = pl.ds(pl.multiple_of(hh * 128, 128), 128)
        for b in range(2):
            n = 256 * (b + 1)
            rows = pl.ds(256 * b, 256)
            seen = pl.ds(0, n)
            p = PR[i, rows, seen]
            grad = AGR[pl.ds(pl.multiple_of(r * 512 + 256 * b, 256), 256), lanes]
            low = score_gradient(p, nt(grad, QKVR[2, i, seen, :]))
            first = r * 2048 + 2 * hh
            WIDE[0, pl.ds(first + 1024 * b, 256, stride=4), :] = nn(low, QKVR[1, i, seen, :]) * SCALE
            dk = tn(low, QKVR[0, i, rows, :])
            dv = tn(p.astype(BF16), grad)
            if b == 0:
                dk_first, dv_first = dk, dv
            else:
                WIDE[1, pl.ds(first, 256, stride=4), :] = (dk[:256] + dk_first) * SCALE
                WIDE[1, pl.ds(first + 1024, 256, stride=4), :] = dk[256:] * SCALE
                WIDE[2, pl.ds(first, 256, stride=4), :] = dv[:256] + dv_first
                WIDE[2, pl.ds(first + 1024, 256, stride=4), :] = dv[256:]
        return carry

    lax.fori_loop(0, 4, row_backward, 0)

    def join_strided(t):
        for copy in dg_in[15 * t : 15 * t + 15]:
            copy.wait_recv()

        def spread(m, carry):
            for hh in range(2):
                block = RDG[t, pl.ds(m * 4, 4), hh].astype(F32)
                for r in range(2):
                    first = r * 2048 + 2 * hh + 1 + m * 512
                    WIDE[t, pl.ds(first, 128, stride=4), :] = block[:, :, 8 * r : 8 * r + 8, :].reshape(128, 128)
            return carry

        lax.fori_loop(0, 4, spread, 0)

        def narrow(m, carry):
            rows = pl.ds(pl.multiple_of(m * 512, 512), 512)
            flat_out[t][rows, :] = WIDE[t, rows, :].astype(BF16)
            return carry

        lax.fori_loop(0, 8, narrow, 0)

    def finish(m, carry):
        rows = pl.ds(pl.multiple_of(m * 256, 256), 256)
        total = LR[3, rows, :].astype(F32) + LX[0, rows, :].astype(F32) + LX[1, rows, :].astype(F32)
        lay_out[rows, :] = total.astype(BF16)
        return carry

    reduce_end(0)
    reduce_end(1)
    join_strided(0)
    join_strided(1)
    for copy in lx_in:
        copy.wait_recv()
    lax.fori_loop(0, 4, finish, 0)
    join_strided(2)
    reduce_end(2)
    reduce_end(3)
    for copy in sends:
        copy.wait_send()


def store(*refs):
    done = refs[10]
    copies = [pltpu.make_async_copy(refs[i], refs[5 + i], done.at[i]) for i in range(5)]
    for copy in copies:
        copy.start()
    for copy in copies:
        copy.wait()


def on_device(queries, keys, values, out_grad, wo):
    flat = tuple(t.reshape(4096, 128) for t in (queries, keys, values))
    flat_shape = pltpu.VMEM((4096, 128), BF16)
    any_spec = pl.BlockSpec(memory_space=pl.ANY)

    def vmem(*shape, dtype=BF16):
        return pltpu.VMEM(shape, dtype)

    def sems(*shape):
        return pltpu.SemaphoreType.DMA(shape)

    out = pl.pallas_call(
        kernel,
        name="layer",
        out_shape=(
            pltpu.VMEM((1024, 512), BF16),
            flat_shape, flat_shape, flat_shape,
            pltpu.VMEM((512, 256), BF16),
        ),
        in_specs=[any_spec] * 5,
        out_specs=[pl.BlockSpec(memory_space=pltpu.VMEM)] * 5,
        scratch_shapes=[
            vmem(3, 4096, 128, dtype=F32),
            vmem(3, 16, 2, 4, 16, 128),
            vmem(3, 16, 2, 4, 16, 128),
            vmem(512, 4096),
            vmem(1024, 4096),
            vmem(3, 4, 512, 128),
            vmem(3, 16, 2, 4, 16, 128),
            vmem(16, 2, 4, 16, 128),
            vmem(16, 2, 4, 16, 128),
            vmem(16, 2, 4, 16, 128),
            vmem(8, 256, 256, dtype=F32),
            vmem(4, 512, 512, dtype=F32),
            vmem(1024, 512),
            vmem(512, 1024),
            vmem(2, 16, 4, 8, 256, dtype=F32),
            vmem(1024, 256),
            vmem(4, 4, 4, 128, 256),
            vmem(4, 2, 2, 128, 256),
            vmem(4, 2, 4, 128, 256),
            vmem(4, 4, 128, 256),
            vmem(4, 3, 128, 256),
            vmem(4, 1024, 512),
            vmem(4, 1024, 512),
            vmem(2, 1024, 512),
            vmem(2, 512, 512),
            sems(8),
            sems(3, 15), sems(3, 15),
            sems(15), sems(15),
            sems(15), sems(15),
            sems(3, 15), sems(3, 15),
            sems(8), sems(8),
            sems(3, 2), sems(3, 2),
            sems(3, 2), sems(3, 2),
            sems(2, 3, 2), sems(2, 3, 2),
            sems(4, 6), sems(4, 6),
            sems(4, 3), sems(4, 3),
            sems(4), sems(4),
            sems(6), sems(6),
        ],
        compiler_params=pltpu.CompilerParams(
            collective_id=0, has_side_effects=True, vmem_limit_bytes=58 << 20
        ),
    )(*flat, out_grad, wo)
    lay, dq, dk, dv, pg = pl.pallas_call(
        store,
        name="store",
        out_shape=tuple(jax.ShapeDtypeStruct(t.shape, t.dtype) for t in out),
        in_specs=[any_spec] * 5,
        out_specs=[any_spec] * 5,
        scratch_shapes=[sems(5)],
        compiler_params=pltpu.CompilerParams(vmem_limit_bytes=1 << 20),
    )(*out)
    return lay, *(t.reshape(1024, 4, 128) for t in (dq, dk, dv)), pg


def solution(mesh):
    in_specs = (
        P("ctx", "head", None),
        P("ctx", "head", None),
        P("ctx", "head", None),
        P("ctx", None),
        P("head", "ctx"),
    )
    out_specs = (
        P("ctx", "head"),
        P("ctx", "head", None),
        P("ctx", "head", None),
        P("ctx", "head", None),
        P("head", "ctx"),
    )
    return jax.shard_map(
        on_device, mesh=mesh, in_specs=in_specs, out_specs=out_specs, check_vma=False
    )
```

```python
import jax
import jax.numpy as jnp
from jax import lax
from jax.experimental import pallas as pl
from jax.experimental.pallas import tpu as pltpu
from jax.sharding import PartitionSpec as P

MESH = pl.DeviceIdType.MESH
BF16 = jnp.bfloat16
F32 = jnp.float32
SCALE = 128 ** -0.5
SEVEN = tuple((dy, dz) for dy in range(4) for dz in range(4) if dy or dz)


def nt(a, b):
    return lax.dot_general(a, b, (((1,), (1,)), ((), ())), preferred_element_type=F32)


def nn(a, b):
    return lax.dot_general(a, b, (((1,), (0,)), ((), ())), preferred_element_type=F32)


def tn(a, b):
    return lax.dot_general(a, b, (((0,), (0,)), ((), ())), preferred_element_type=F32)


def softmax(scores, visible):
    scores = jnp.where(visible, scores * SCALE, -jnp.inf)
    lifted = jnp.exp(scores - jnp.max(scores, axis=-1, keepdims=True))
    return lifted / jnp.sum(lifted, axis=-1, keepdims=True)


def score_gradient(p, dp):
    return (p * (dp - jnp.sum(p * dp, axis=-1, keepdims=True))).astype(BF16)


def kernel(
    q_hbm, k_hbm, v_hbm, og_hbm, wo_hbm,
    lay_out, dq_out, dk_out, dv_out, pg_out,
    WIDE, QS, RDG,
    W, OG, QKVR, REC, RDO, SO, RO, PC, PR, ATT, ATTT, AGF, AGR, PP, RL, R1, S2, R2, LS, LR, LX, XR,
    loc, qkv_s, qkv_r, o_s, o_r, do_s, do_r, dg_s, dg_r, w1_s, w1_r, wa_s, wa_r, wb_s, wb_r, wc_s, wc_r,
    p1_s, p1_r, p2_s, p2_r, lp_s, lp_r, lx_s, lx_r,
):
    c = lax.axis_index("ctx")
    h = lax.axis_index("head")
    y, z = c // 4, lax.rem(c, 4)
    x, core = h // 2, lax.rem(h, 2)

    def grid_peer(dy, dz):
        return lax.rem(y + dy, 4) * 4 + lax.rem(z + dz, 4)

    def x_head(dx):
        return lax.rem(x + dx, 4) * 2 + core

    partner = (c, x * 2 + (1 - core))

    def remote(src, dst, ssem, rsem, dev):
        return pltpu.make_async_remote_copy(
            src_ref=src, dst_ref=dst, send_sem=ssem, recv_sem=rsem, device_id=dev, device_id_type=MESH
        )

    sends = []

    def push(copy):
        copy.start()
        sends.append(copy)
        return copy

    def drain(copies):
        for copy in copies:
            copy.wait_send()
            sends[:] = [other for other in sends if other is not copy]

    flat_out = (dq_out, dk_out, dv_out)
    own_cols = pl.ds(pl.multiple_of(c * 256, 256), 256)

    loads_q = []
    for t, src in enumerate((q_hbm, k_hbm, v_hbm)):
        copy = pltpu.make_async_copy(src, flat_out[t], loc.at[t])
        copy.start()
        loads_q.append(copy)
    loads_w = []
    for slot, j in enumerate((0, 2, 1, 3)):
        copy = pltpu.make_async_copy(
            wo_hbm.at[pl.ds(j * 128, 128)], W.at[pl.ds(slot * 128, 128), own_cols], loc.at[3 + slot]
        )
        copy.start()
        loads_w.append(copy)
    load_og = pltpu.make_async_copy(og_hbm, OG, loc.at[7])
    load_og.start()

    barrier = pltpu.get_barrier_semaphore()
    for dy, dz in SEVEN:
        pl.semaphore_signal(barrier, inc=1, device_id=(grid_peer(dy, dz), h), device_id_type=MESH)
    for dx in range(1, 4):
        pl.semaphore_signal(barrier, inc=1, device_id=(c, x_head(dx)), device_id_type=MESH)
    pl.semaphore_signal(barrier, inc=1, device_id=partner, device_id_type=MESH)

    def unpack(t):
        loads_q[t].wait()

        def widen(m, carry):
            rows = pl.ds(pl.multiple_of(m * 512, 512), 512)
            WIDE[t, rows, :] = flat_out[t][rows, :].astype(F32)
            return carry

        lax.fori_loop(0, 8, widen, 0)

        def strided(m, carry):
            for hh in range(2):
                both = []
                for r in range(2):
                    first = r * 2048 + 2 * hh + 1 + m * 512
                    both.append(WIDE[t, pl.ds(first, 128, stride=4), :].reshape(4, 4, 8, 128))
                QS[t, pl.ds(m * 4, 4), hh] = jnp.concatenate(both, axis=2).astype(BF16)
            return carry

        lax.fori_loop(0, 4, strided, 0)

    unpack(0)
    for copy in loads_w:
        copy.wait()
    pl.semaphore_wait(barrier, 19)

    qkv_in = []

    def send_strided(t):
        for i, (dy, dz) in enumerate(SEVEN):
            to = grid_peer(dy, dz)
            qkv_in.append(push(remote(QS.at[t, to], REC.at[t, c], qkv_s.at[t, i], qkv_r.at[t, i], (to, h))))
        REC[t, c] = QS[t, c]

    send_strided(0)
    unpack(1)
    send_strided(1)
    w_own = W.at[:, own_cols]
    wz, wy = {}, {}
    for k, d in enumerate((1, 3)):
        wz[d] = push(remote(w_own, w_own, w1_s.at[k], w1_r.at[k], (grid_peer(0, d), h)))
        wy[d] = push(remote(w_own, w_own, w1_s.at[2 + k], w1_r.at[2 + k], (grid_peer(d, 0), h)))
    unpack(2)
    send_strided(2)

    def w_block(first, size, owner):
        return W.at[pl.ds(first, size), pl.ds(pl.multiple_of(owner * 256, 256), 256)]

    wa = [[None] * 2 for _ in range(3)]
    wb = [[None] * 2 for _ in range(3)]
    wr = []

    def spread_along(d):
        block = w_block(0, 256, grid_peer(0, 4 - d))
        for k, e in enumerate((1, 3)):
            wa[d - 1][k] = push(remote(block, block, wa_s.at[d - 1, k], wa_r.at[d - 1, k], (grid_peer(e, 0), h)))
        block = w_block(256, 256, grid_peer(4 - d, 0))
        for k, e in enumerate((1, 3)):
            wb[d - 1][k] = push(remote(block, block, wb_s.at[d - 1, k], wb_r.at[d - 1, k], (grid_peer(0, e), h)))

    def spread_w():
        for d in (1, 3):
            wz[d].wait_recv()
            wy[d].wait_recv()
        for k, (first, dy, dz) in enumerate(((0, 0, 1), (256, 0, 3), (256, 1, 0), (0, 3, 0))):
            block = w_block(first, 256, grid_peer((4 - dy) % 4, (4 - dz) % 4))
            wr.append(push(remote(block, block, w1_s.at[4 + k], w1_r.at[4 + k], (grid_peer(dy, dz), h))))
        spread_along(1)
        spread_along(3)

    def spread_far():
        for copy in wr:
            copy.wait_recv()
        spread_along(2)

    wc = []

    def relay_w(d):
        for k, e in enumerate((1, 3)):
            wa[d - 1][k].wait_recv()
            block = w_block(128 * k, 128, grid_peer(4 - e, 4 - d))
            wc.append(push(remote(block, block, wc_s.at[0, d - 1, k], wc_r.at[0, d - 1, k], (grid_peer(e, 0), h))))
            wb[d - 1][k].wait_recv()
            block = w_block(256 + 128 * k, 128, grid_peer(4 - d, 4 - e))
            wc.append(push(remote(block, block, wc_s.at[1, d - 1, k], wc_r.at[1, d - 1, k], (grid_peer(0, e), h))))

    def unpack_rows(m, carry):
        for t in range(3):
            for hh in range(2):
                rows = WIDE[t, pl.ds(m * 512 + 2 * hh, 128, stride=4), :].astype(BF16)
                QKVR[t, (m // 4) * 2 + hh, pl.ds(pl.multiple_of(lax.rem(m, 4) * 128, 128), 128), :] = rows
        return carry

    lax.fori_loop(0, 8, unpack_rows, 0)

    def causal(rows, cols, first):
        return (
            lax.broadcasted_iota(jnp.int32, (rows, cols), 0) + first
            >= lax.broadcasted_iota(jnp.int32, (rows, cols), 1)
        )

    def row_forward(i, carry):
        r, hh = i // 2, lax.rem(i, 2)
        lanes = pl.ds(pl.multiple_of(hh * 128, 128), 128)
        for b in range(2):
            n = 256 * (b + 1)
            q = QKVR[0, i, pl.ds(256 * b, 256), :]
            p = softmax(nt(q, QKVR[1, i, pl.ds(0, n), :]), causal(256, n, 256 * b))
            PR[i, pl.ds(256 * b, 256), pl.ds(0, n)] = p
            o = nn(p.astype(BF16), QKVR[2, i, pl.ds(0, n), :])
            rows = pl.ds(pl.multiple_of(r * 512 + 256 * b, 256), 256)
            ATT[rows, lanes] = o.astype(BF16)
            ATTT[lanes, rows] = o.T.astype(BF16)
        return carry

    lax.fori_loop(0, 4, row_forward, 0)

    def projection(half):
        def one(n, carry):
            cols = pl.ds(pl.multiple_of(n * 256, 256), 256)
            part = nn(ATTT[pl.ds(256 * half, 256), :], OG[:, cols])
            for q in range(2):
                PP[2 * half + q, n // 4, lax.rem(n, 4)] = part[128 * q : 128 * q + 128].astype(BF16)
            return carry

        lax.fori_loop(0, 16, one, 0)

    load_og.wait()
    projection(0)
    spread_w()

    first_half, second_half = pl.ds(0, 2), pl.ds(2, 2)

    def group(q, d, part):
        if q % 2 == 0:
            return PP.at[q, part, lax.rem(z + d, 4)]
        return PP.at[q, lax.rem(y + d, 4), part]

    def along(q, d, second=False):
        return (grid_peer(0, d) if (q % 2 == 0) != second else grid_peer(d, 0), h)

    pr_in, p1_in, p2_in = [None] * 4, [None] * 4, [None] * 4

    def reduce_start(q):
        pr_in[q] = [
            push(remote(group(q, 2, first_half), RL.at[q, 0], p1_s.at[q, 0], p1_r.at[q, 0], along(q, 1))),
            push(remote(group(q, 2, second_half), RL.at[q, 1], p1_s.at[q, 1], p1_r.at[q, 1], along(q, 3))),
        ]
        p1_in[q] = [
            push(remote(group(q, 1, second_half), R1.at[q, 0, second_half], p1_s.at[q, 2], p1_r.at[q, 2], along(q, 1))),
            push(remote(group(q, 3, first_half), R1.at[q, 1, first_half], p1_s.at[q, 3], p1_r.at[q, 3], along(q, 3))),
        ]

    def reduce_pass(q):
        for k, (d, part) in enumerate(((1, first_half), (3, second_half))):
            pr_in[q][k].wait_recv()
            mine = group(q, d, part)
            mine[...] = (mine[...].astype(F32) + RL[q, k].astype(F32)).astype(BF16)
            p1_in[q].append(
                push(remote(mine, R1.at[q, k, part], p1_s.at[q, 4 + k], p1_r.at[q, 4 + k], along(q, d)))
            )

    def reduce_middle(q):
        for copy in p1_in[q]:
            copy.wait_recv()
        p2_in[q] = []
        for d in (2, 1, 3, 0):
            if q % 2 == 0:
                other = lax.rem(y + d, 4)
                mine = PP[q, other, z]
            else:
                other = lax.rem(z + d, 4)
                mine = PP[q, y, other]
            total = mine.astype(F32) + R1[q, 0, other].astype(F32) + R1[q, 1, other].astype(F32)
            S2[q, d] = total.astype(BF16)
            if d:
                p2_in[q].append(
                    push(remote(S2.at[q, d], R2.at[q, d - 1], p2_s.at[q, d - 1], p2_r.at[q, d - 1], along(q, d, True)))
                )

    def reduce_end(q):
        for copy in p2_in[q]:
            copy.wait_recv()
        total = S2[q, 0].astype(F32)
        for k in range(3):
            total = total + R2[q, k].astype(F32)
        pg_out[pl.ds((2 * (q % 2) + q // 2) * 128, 128), :] = total.astype(BF16)

    for copy in qkv_in:
        copy.wait_recv()
    ii = lax.broadcasted_iota(jnp.int32, (256, 256), 0)
    jj = lax.broadcasted_iota(jnp.int32, (256, 256), 1)

    def tile(ref):
        return ref.reshape(256, 128)

    def col_forward(i, carry):
        hh, g = i // 4, lax.rem(i, 4)
        visible = (lax.rem(ii, 8) == lax.rem(jj, 8)) & (ii >= jj)
        p = softmax(nt(tile(REC[0, :, hh, g]), tile(REC[1, :, hh, g])), visible)
        PC[i] = p
        o = nn(p.astype(BF16), tile(REC[2, :, hh, g]))
        SO[:, hh, g] = o.astype(BF16).reshape(16, 16, 128)
        return carry

    lax.fori_loop(0, 8, col_forward, 0, unroll=2)
    spread_far()
    o_in = []
    for i, (dy, dz) in enumerate(SEVEN):
        to = grid_peer(dy, dz)
        o_in.append(push(remote(SO.at[to], RO.at[c], o_s.at[i], o_r.at[i], (to, h))))
    RO[c] = SO[c]

    relay_w(1)
    relay_w(3)
    relay_w(2)
    reduce_start(0)
    reduce_start(1)

    for copy in o_in:
        copy.wait_recv()
    for hh in range(2):
        for g in range(4):
            block = RO[:, hh, g].astype(F32)
            for r in range(2):
                AGF[r, :, g, :, pl.ds(hh * 128, 128)] = block[:, 8 * r : 8 * r + 8, :]

    def place(m, carry):
        block = AGF[m // 2, pl.ds(pl.multiple_of(lax.rem(m, 2) * 8, 8), 8)].reshape(256, 256)
        rows = pl.ds(pl.multiple_of(m * 256, 256), 256)
        ATT[rows, pl.ds(256, 256)] = block.astype(BF16)
        ATTT[pl.ds(256, 256), rows] = block.T.astype(BF16)
        return carry

    lax.fori_loop(0, 4, place, 0)
    projection(1)
    reduce_start(2)
    reduce_start(3)

    for copy in wc:
        copy.wait_recv()

    def partial_out(m, head):
        rows = pl.ds(pl.multiple_of(m * 256, 256), 256)
        cols = pl.ds(pl.multiple_of(head * 512, 512), 512)
        return rows, nn(ATT[rows, :], W[:, cols])

    order = (2, 1, 3, 0)
    lp_in = [None] * 4

    def to_partner(n):
        head = lax.rem(x + order[n], 4) * 2 + (1 - core)

        def for_partner(m, carry):
            rows, part = partial_out(m, head)
            LS[n, rows, :] = part.astype(BF16)
            return carry

        lax.fori_loop(0, 4, for_partner, 0)
        lp_in[n] = push(remote(LS.at[n], LR.at[n], lp_s.at[n], lp_r.at[n], partner))

    def to_x(n):
        head = x_head(order[n])
        lp_in[n].wait_recv()

        def for_x(m, carry):
            rows, part = partial_out(m, head)
            LR[n, rows, :] = (part + LR[n, rows, :].astype(F32)).astype(BF16)
            return carry

        lax.fori_loop(0, 4, for_x, 0)

    lower, upper = pl.ds(0, 512), pl.ds(512, 512)
    ahead, behind = (c, x_head(1)), (c, x_head(3))

    def add_passing(n, k, rows):
        relay[k].wait_recv()
        LR[n, rows, :] = (LR[n, rows, :].astype(F32) + XR[k].astype(F32)).astype(BF16)

    def add_x():
        add_passing(1, 0, lower)
        lx_in.append(push(remote(LR.at[1, lower], LX.at[0, lower], lx_s.at[4], lx_r.at[4], ahead)))
        add_passing(2, 1, upper)
        lx_in.append(push(remote(LR.at[2, upper], LX.at[1, upper], lx_s.at[5], lx_r.at[5], behind)))

    to_partner(0)
    to_partner(1)
    to_x(0)
    relay = [
        push(remote(LR.at[0, lower], XR.at[0], lx_s.at[0], lx_r.at[0], ahead)),
        push(remote(LR.at[0, upper], XR.at[1], lx_s.at[1], lx_r.at[1], behind)),
    ]

    def strided_cotangent(m, carry):
        rows = pl.ds(pl.multiple_of(m * 256, 256), 256)
        part = nt(OG[rows, :], W[pl.ds(256, 256), :])
        AGF[m // 2, pl.ds(pl.multiple_of(lax.rem(m, 2) * 8, 8), 8)] = part.reshape(8, 4, 8, 256)
        return carry

    lax.fori_loop(0, 4, strided_cotangent, 0)
    drain(o_in)
    for hh in range(2):
        for g in range(4):
            lanes = pl.ds(hh * 128, 128)
            both = jnp.concatenate([AGF[0, :, g, :, lanes], AGF[1, :, g, :, lanes]], axis=1)
            SO[:, hh, g] = both.astype(BF16)
    do_in = []
    for i, (dy, dz) in enumerate(SEVEN):
        to = grid_peer(dy, dz)
        do_in.append(push(remote(SO.at[to], RDO.at[c], do_s.at[i], do_r.at[i], (to, h))))
    RDO[c] = SO[c]
    reduce_pass(0)
    reduce_pass(1)

    to_partner(2)
    to_x(1)
    lx_in = [push(remote(LR.at[1, upper], LX.at[0, upper], lx_s.at[2], lx_r.at[2], ahead))]
    to_partner(3)
    to_x(2)
    lx_in.append(push(remote(LR.at[2, lower], LX.at[1, lower], lx_s.at[3], lx_r.at[3], behind)))

    reduce_pass(2)
    reduce_pass(3)
    to_x(3)

    def row_cotangent(m, carry):
        rows = pl.ds(pl.multiple_of(m * 256, 256), 256)
        AGR[rows, :] = nt(OG[rows, :], W[pl.ds(0, 256), :]).astype(BF16)
        return carry

    lax.fori_loop(0, 4, row_cotangent, 0)
    reduce_middle(0)
    reduce_middle(1)

    for copy in do_in:
        copy.wait_recv()

    def col_backward(i, carry):
        hh, g = i // 4, lax.rem(i, 4)
        p = PC[i]
        grad = tile(RDO[:, hh, g])
        low = score_gradient(p, nt(grad, tile(REC[2, :, hh, g])))
        QS[0, :, hh, g] = (nn(low, tile(REC[1, :, hh, g])) * SCALE).astype(BF16).reshape(16, 16, 128)
        QS[1, :, hh, g] = (tn(low, tile(REC[0, :, hh, g])) * SCALE).astype(BF16).reshape(16, 16, 128)
        QS[2, :, hh, g] = tn(p.astype(BF16), grad).astype(BF16).reshape(16, 16, 128)
        return carry

    drain(qkv_in)
    lax.fori_loop(0, 8, col_backward, 0, unroll=2)
    dg_in = []
    for t in range(3):
        for i, (dy, dz) in enumerate(SEVEN):
            to = grid_peer(dy, dz)
            dg_in.append(push(remote(QS.at[t, to], RDG.at[t, c], dg_s.at[t, i], dg_r.at[t, i], (to, h))))
        RDG[t, c] = QS[t, c]

    add_x()
    reduce_middle(2)
    reduce_middle(3)

    def row_backward(i, carry):
        r, hh = i // 2, lax.rem(i, 2)
        lanes = pl.ds(pl.multiple_of(hh * 128, 128), 128)
        for b in range(2):
            n = 256 * (b + 1)
            rows = pl.ds(256 * b, 256)
            seen = pl.ds(0, n)
            p = PR[i, rows, seen]
            grad = AGR[pl.ds(pl.multiple_of(r * 512 + 256 * b, 256), 256), lanes]
            low = score_gradient(p, nt(grad, QKVR[2, i, seen, :]))
            first = r * 2048 + 2 * hh
            WIDE[0, pl.ds(first + 1024 * b, 256, stride=4), :] = nn(low, QKVR[1, i, seen, :]) * SCALE
            dk = tn(low, QKVR[0, i, rows, :])
            dv = tn(p.astype(BF16), grad)
            if b == 0:
                dk_first, dv_first = dk, dv
            else:
                WIDE[1, pl.ds(first, 256, stride=4), :] = (dk[:256] + dk_first) * SCALE
                WIDE[1, pl.ds(first + 1024, 256, stride=4), :] = dk[256:] * SCALE
                WIDE[2, pl.ds(first, 256, stride=4), :] = dv[:256] + dv_first
                WIDE[2, pl.ds(first + 1024, 256, stride=4), :] = dv[256:]
        return carry

    lax.fori_loop(0, 4, row_backward, 0)

    def join_strided(t):
        for copy in dg_in[15 * t : 15 * t + 15]:
            copy.wait_recv()

        def spread(m, carry):
            for hh in range(2):
                block = RDG[t, pl.ds(m * 4, 4), hh].astype(F32)
                for r in range(2):
                    first = r * 2048 + 2 * hh + 1 + m * 512
                    WIDE[t, pl.ds(first, 128, stride=4), :] = block[:, :, 8 * r : 8 * r + 8, :].reshape(128, 128)
            return carry

        lax.fori_loop(0, 4, spread, 0)

        def narrow(m, carry):
            rows = pl.ds(pl.multiple_of(m * 512, 512), 512)
            flat_out[t][rows, :] = WIDE[t, rows, :].astype(BF16)
            return carry

        lax.fori_loop(0, 8, narrow, 0)

    def finish(m, carry):
        rows = pl.ds(pl.multiple_of(m * 256, 256), 256)
        total = LR[3, rows, :].astype(F32) + LX[0, rows, :].astype(F32) + LX[1, rows, :].astype(F32)
        lay_out[rows, :] = total.astype(BF16)
        return carry

    join_strided(0)
    join_strided(1)
    for copy in lx_in:
        copy.wait_recv()
    lax.fori_loop(0, 4, finish, 0)
    join_strided(2)
    reduce_end(0)
    reduce_end(1)
    reduce_end(2)
    reduce_end(3)
    for copy in sends:
        copy.wait_send()


def store(*refs):
    done = refs[10]
    copies = [pltpu.make_async_copy(refs[i], refs[5 + i], done.at[i]) for i in range(5)]
    for copy in copies:
        copy.start()
    for copy in copies:
        copy.wait()


def on_device(queries, keys, values, out_grad, wo):
    flat = tuple(t.reshape(4096, 128) for t in (queries, keys, values))
    flat_shape = pltpu.VMEM((4096, 128), BF16)
    any_spec = pl.BlockSpec(memory_space=pl.ANY)

    def vmem(*shape, dtype=BF16):
        return pltpu.VMEM(shape, dtype)

    def sems(*shape):
        return pltpu.SemaphoreType.DMA(shape)

    out = pl.pallas_call(
        kernel,
        name="layer",
        out_shape=(
            pltpu.VMEM((1024, 512), BF16),
            flat_shape, flat_shape, flat_shape,
            pltpu.VMEM((512, 256), BF16),
        ),
        in_specs=[any_spec] * 5,
        out_specs=[pl.BlockSpec(memory_space=pltpu.VMEM)] * 5,
        scratch_shapes=[
            vmem(3, 4096, 128, dtype=F32),
            vmem(3, 16, 2, 4, 16, 128),
            vmem(3, 16, 2, 4, 16, 128),
            vmem(512, 4096),
            vmem(1024, 4096),
            vmem(3, 4, 512, 128),
            vmem(3, 16, 2, 4, 16, 128),
            vmem(16, 2, 4, 16, 128),
            vmem(16, 2, 4, 16, 128),
            vmem(16, 2, 4, 16, 128),
            vmem(8, 256, 256, dtype=F32),
            vmem(4, 512, 512, dtype=F32),
            vmem(1024, 512),
            vmem(512, 1024),
            vmem(2, 16, 4, 8, 256, dtype=F32),
            vmem(1024, 256),
            vmem(4, 4, 4, 128, 256),
            vmem(4, 2, 2, 128, 256),
            vmem(4, 2, 4, 128, 256),
            vmem(4, 4, 128, 256),
            vmem(4, 3, 128, 256),
            vmem(4, 1024, 512),
            vmem(4, 1024, 512),
            vmem(2, 1024, 512),
            vmem(2, 512, 512),
            sems(8),
            sems(3, 15), sems(3, 15),
            sems(15), sems(15),
            sems(15), sems(15),
            sems(3, 15), sems(3, 15),
            sems(8), sems(8),
            sems(3, 2), sems(3, 2),
            sems(3, 2), sems(3, 2),
            sems(2, 3, 2), sems(2, 3, 2),
            sems(4, 6), sems(4, 6),
            sems(4, 3), sems(4, 3),
            sems(4), sems(4),
            sems(6), sems(6),
        ],
        compiler_params=pltpu.CompilerParams(
            collective_id=0, has_side_effects=True, vmem_limit_bytes=58 << 20
        ),
    )(*flat, out_grad, wo)
    lay, dq, dk, dv, pg = pl.pallas_call(
        store,
        name="store",
        out_shape=tuple(jax.ShapeDtypeStruct(t.shape, t.dtype) for t in out),
        in_specs=[any_spec] * 5,
        out_specs=[any_spec] * 5,
        scratch_shapes=[sems(5)],
        compiler_params=pltpu.CompilerParams(vmem_limit_bytes=1 << 20),
    )(*out)
    return lay, *(t.reshape(1024, 4, 128) for t in (dq, dk, dv)), pg


def solution(mesh):
    in_specs = (
        P("ctx", "head", None),
        P("ctx", "head", None),
        P("ctx", "head", None),
        P("ctx", None),
        P("head", "ctx"),
    )
    out_specs = (
        P("ctx", "head"),
        P("ctx", "head", None),
        P("ctx", "head", None),
        P("ctx", "head", None),
        P("head", "ctx"),
    )
    return jax.shard_map(
        on_device, mesh=mesh, in_specs=in_specs, out_specs=out_specs, check_vma=False
    )
```
